256 devices in a mesh: seq: 32 (over x, z), expert: 8 (over y, core).
Axes of the slice: x: 4, y: 4, z: 8, core: 2. Of those that a mesh axis runs over, the one named last changes fastest.
Arguments:
- byte_states: bfloat16 [65536, 512], P(('seq', 'expert')), may hold values from -6 to 6
- patch_start: int32 [65536], P(('seq', 'expert')), may hold values from 0 to 1, as said below
- expert_ids: int32 [10240, 2], P(('seq', 'expert')), may hold values from 0 to 7, all different within a row; in each aligned block of 40 rows (0 to 39, 40 to 79, ...) at most 12 rows name the same one
- enc_gain: float32 [512], replicated, may hold values from 0.1 to 1.9
- w_qkv: bfloat16 [512, 1536], replicated, may hold values from -0.25 to 0.25
- w_out: bfloat16 [512, 512], replicated, may hold values from -0.25 to 0.25
- w_xq: bfloat16 [512, 512], replicated, may hold values from -0.25 to 0.25
- w_xkv: bfloat16 [512, 1024], replicated, may hold values from -0.25 to 0.25
- w_up: bfloat16 [512, 2048], replicated, may hold values from -0.25 to 0.25
- moe_gain: float32 [2048], replicated, may hold values from 0.1 to 1.9
- w_router: float32 [2048, 8], replicated, may hold values from -0.03125 to 0.03125
- w_in: bfloat16 [8, 2048, 2, 6144], P('expert', None, None, 'seq'), may hold values from -0.125 to 0.125
- w_down: bfloat16 [8, 6144, 2048], P('expert', 'seq'), may hold values from -0.15625 to 0.15625
- dec_gain: float32 [512], replicated, may hold values from 0.1 to 1.9
- w_dq: bfloat16 [512, 512], replicated, may hold values from -0.25 to 0.25
- w_dkv: bfloat16 [2048, 1024], replicated, may hold values from -0.125 to 0.125
- w_do: bfloat16 [512, 512], replicated, may hold values from -0.25 to 0.25
Outputs:
- bytes_out: bfloat16 [65536, 512], P(('seq', 'expert'))
- patch_out: bfloat16 [10240, 2048], P(('seq', 'expert'))
The draws below stay inside these ranges and needn't reach their ends.
Inputs may be any that keep to these rules, and one draw needn't show every extreme that they name: `patch_start`: the first byte of every block of 256 bytes has a 1; every block has between 20 and 40 ones, and some block has exactly 40. `expert_ids`: the two experts of a slot differ. Among the 80 entries of one block's slots no expert appears more than 12 times, and some expert appears exactly 12 times in some block.
All inputs are finite; a program needn't handle non-finite values.
Results may differ from the reference program's by a relative error of at most 0.025.
Values may be sent and summed in bfloat16 or wider, within the bound.
A program may use at most 128 MiB of HBM per device.

```python
import math
import jax
import jax.numpy as jnp
import numpy as np
from jax import lax

DL = 512
HEADS_L = 8
HEAD = 64
WINDOW = 512
DG = 2048
FF = 6144
BYTE_DEV = 256
EXPERTS = 8
PATCH_CAP = 40
CAP = 12
BYTES = 65536
PATCHES = 10240
N_SEQ = 32


def draw_patch_start(key, part):
    devices = BYTES // BYTE_DEV
    first, second, third = jax.random.split(key, 3)
    counts = jax.random.randint(first, (devices,), PATCH_CAP // 2, PATCH_CAP + 1)
    fullest = jax.random.randint(second, (), 0, devices)
    counts = jnp.where(jnp.arange(devices) == fullest, PATCH_CAP, counts)
    scores = jax.random.randint(third, (devices, BYTE_DEV - 1), 0, 1 << 20) * BYTE_DEV + jnp.arange(BYTE_DEV - 1)
    ordering = jnp.argsort(scores, axis=1)
    ranking = jnp.argsort(ordering, axis=1)
    inner = (ranking < counts[:, None] - 1).astype(jnp.int32)
    flags = jnp.concatenate([jnp.ones((devices, 1), jnp.int32), inner], axis=1)
    return flags.reshape(-1).astype(jnp.int32)


def steps_of(key, shape, cuts, least, largest):
    level, own = 1.0, jax.random.fold_in(key, 6)
    for axis_at, blocks in cuts:
        steps = jnp.exp(jax.random.uniform(jax.random.fold_in(own, axis_at), (blocks,), jnp.float32, least / len(cuts), largest / len(cuts)))
        level = level * jnp.repeat(steps, shape[axis_at] // blocks).reshape([-1 if axis == axis_at else 1 for axis in range(len(shape))])
    return level


def assign_block(key, own, number, rows, amount, top, most, skew):
    order = jax.random.permutation(key, amount)
    heavy_load, common = load_shares(amount, rows * top, most, skew, True), load_shares(amount, rows * top, most, skew, False)
    places = jnp.arange(amount)

    def named(tallies, turn):
        used = int((tallies > 0).sum())
        fixed = max(1, used // 4)
        shifted = fixed + (places - fixed + turn * (used - fixed)) % max(1, amount - fixed)
        return jnp.zeros((amount,), jnp.int32).at[order[jnp.where(places < fixed, places, shifted)]].set(jnp.asarray(tallies, jnp.int32))

    tallies = jnp.where(number % 4 == 0, named(heavy_load, number // 4), named(common, number - number // 4 - 1))
    mixed = jax.random.permutation(jax.random.fold_in(own, 3), amount)
    donor, sink = mixed[0:amount // 2 * 2:2], mixed[1:amount // 2 * 2:2]
    room = jnp.minimum(tallies[donor] - 1, most - tallies[sink]) // 2
    room = jnp.where((donor == order[0]) | (sink == order[0]) | (tallies[sink] == 0), 0, jnp.maximum(room, 0))
    shifted = jax.random.randint(jax.random.fold_in(own, 4), (amount // 2,), 0, 1 << 20) % (room + 1)
    tallies = tallies.at[donor].add(-shifted).at[sink].add(shifted)
    items = jnp.searchsorted(jnp.cumsum(tallies), jnp.arange(rows * top), side="right").astype(jnp.int32)
    grid = items.reshape(top, rows).T
    grid = grid[jax.random.permutation(jax.random.fold_in(own, 1), rows)]
    turn = jax.random.randint(jax.random.fold_in(own, 2), (rows, 1), 0, top)
    return jnp.take_along_axis(grid, (jnp.arange(top)[None, :] + turn) % top, axis=1)


def load_shares(number_of, total, bound, lean, full):
    weights = [(1 << 20) // math.isqrt(standing ** lean) + 1 for standing in range(1, number_of + 1)]
    largest = bound if full else min(bound, max(-(-total // number_of), total * weights[0] // sum(weights)))
    least = 1 if total - largest >= number_of - 1 else 0
    given, surplus = [largest] + [least] * (number_of - 1), total - largest - least * (number_of - 1)
    while surplus > 0:
        movable = [i for i in range(1, number_of) if given[i] < largest] or [i for i in range(1, number_of) if given[i] < bound]
        mass, budget = sum([weights[i] for i in movable]), surplus
        for i in movable:
            addition = min(bound - given[i], max(1, budget * weights[i] // mass), surplus)
            given[i] = given[i] + addition
            surplus = surplus - addition
    return np.array(given)


def gaussian(key, shape, spread, bound, pieces=(), held_as=jnp.bfloat16):
    level = steps_of(key, shape, pieces, -0.22, 0.18) if pieces else 1.0
    drawn = jax.random.normal(key, shape, jnp.float32) * spread * level
    return jnp.minimum(jnp.maximum(drawn, -bound), bound).astype(held_as)


def setup_inputs(seed: int = 0) -> dict:
    seeds = jax.random.split(jax.random.key(seed), 18)
    byte_states = gaussian(seeds[0], (BYTES, DL), 1.0, 6.0, ((0, 256),))
    patch_start = draw_patch_start(jax.random.fold_in(seeds[17], 71), 0)
    expert_ids_keys = jax.random.split(jax.random.fold_in(seeds[2], 1), PATCHES // PATCH_CAP)
    expert_ids_turns = jax.random.permutation(jax.random.fold_in(seeds[2], 3), PATCHES // PATCH_CAP)
    expert_ids = jax.vmap(lambda own, number: assign_block(jax.random.fold_in(seeds[2], 2), own, number, PATCH_CAP, EXPERTS, 2, CAP, 2))(expert_ids_keys, expert_ids_turns).reshape((PATCHES, 2))
    enc_gain = jnp.clip(1.0 + 0.18 * jax.random.normal(seeds[3], (DL,), jnp.float32), 0.1, 1.9)
    w_qkv = gaussian(seeds[4], (DL, 3 * DL), DL ** -0.5, 0.25)
    w_out = gaussian(seeds[5], (DL, DL), DL ** -0.5, 0.25)
    w_xq = gaussian(seeds[6], (DL, DL), DL ** -0.5, 0.25)
    w_xkv = gaussian(seeds[7], (DL, 2 * DL), DL ** -0.5, 0.25)
    w_up = gaussian(seeds[8], (DL, DG), DL ** -0.5, 0.25)
    moe_gain = jnp.clip(1.0 + 0.18 * jax.random.normal(seeds[9], (DG,), jnp.float32), 0.1, 1.9)
    w_router = gaussian(seeds[10], (DG, EXPERTS), (DG * 16) ** -0.5, 0.03125, (), jnp.float32)
    w_in = gaussian(seeds[11], (EXPERTS, DG, 2, FF), DG ** -0.5, 0.125, ((0, 8), (3, 32)))
    w_down = gaussian(seeds[12], (EXPERTS, FF, DG), (FF // 4) ** -0.5, 0.15625, ((0, 8), (1, 32)))
    dec_gain = jnp.clip(1.0 + 0.18 * jax.random.normal(seeds[13], (DL,), jnp.float32), 0.1, 1.9)
    w_dq = gaussian(seeds[14], (DL, DL), DL ** -0.5, 0.25)
    w_dkv = gaussian(seeds[15], (DG, 2 * DL), DG ** -0.5, 0.125)
    w_do = gaussian(seeds[16], (DL, DL), DL ** -0.5, 0.25)
    return dict(byte_states=byte_states, patch_start=patch_start, expert_ids=expert_ids, enc_gain=enc_gain, w_qkv=w_qkv, w_out=w_out, w_xq=w_xq, w_xkv=w_xkv, w_up=w_up, moe_gain=moe_gain, w_router=w_router, w_in=w_in, w_down=w_down, dec_gain=dec_gain, w_dq=w_dq, w_dkv=w_dkv, w_do=w_do)


epsilon = 1e-06
very_negative = -1e+30

def rms_scale(inputs, gain_vector):
    widened = inputs.astype(jnp.float32)
    return widened * lax.rsqrt(lax.optimization_barrier(jnp.mean(widened * widened, axis=-1, keepdims=True)) + epsilon) * gain_vector

def softmax_rows(scores):
    highest = lax.optimization_barrier(jnp.max(scores, axis=-1, keepdims=True))
    raised = jnp.exp(scores - highest)
    return raised / lax.optimization_barrier(jnp.sum(raised, axis=-1, keepdims=True))

def heads_split(inputs):
    return inputs.reshape(inputs.shape[0], HEADS_L, HEAD).transpose(1, 0, 2)

def heads_merge(inputs):
    return inputs.transpose(1, 0, 2).reshape(inputs.shape[1], HEADS_L * HEAD)

def attend(queries, keys, values, allowed):
    scores = jnp.einsum('hqd,hkd->hqk', queries.astype(jnp.float32), keys.astype(jnp.float32)) / math.sqrt(HEAD)
    scores = jnp.where(allowed[None], scores, very_negative)
    weights = softmax_rows(scores).astype(jnp.bfloat16)
    mixed = jnp.einsum('hqk,hkd->hqd', weights.astype(jnp.float32), values.astype(jnp.float32))
    return heads_merge(mixed)

def window_mask(query_place, key_place):
    later = key_place[None, :]
    return (later >= 0) & (later <= query_place[:, None]) & (later > query_place[:, None] - WINDOW)

def encoder(byte_states, enc_gain, w_qkv, w_out):
    normed = rms_scale(byte_states, enc_gain).astype(jnp.bfloat16)
    projected = jnp.dot(normed, w_qkv, preferred_element_type=jnp.float32).astype(jnp.bfloat16)
    padding = jnp.zeros((WINDOW, 2 * DL), projected.dtype)
    pairs = jnp.concatenate([padding, projected[:, DL:]], axis=0)

    def one_block(block_index):
        offset = (block_index * BYTE_DEV).astype(jnp.int32)
        queries = lax.dynamic_slice_in_dim(projected, offset, BYTE_DEV, 0)[:, :DL]
        nearby = lax.dynamic_slice_in_dim(pairs, offset, BYTE_DEV + WINDOW, 0)
        query_place = offset + jnp.arange(BYTE_DEV, dtype=jnp.int32)
        key_place = offset - WINDOW + jnp.arange(BYTE_DEV + WINDOW, dtype=jnp.int32)
        mixed = attend(heads_split(queries), heads_split(nearby[:, :DL]), heads_split(nearby[:, DL:]), window_mask(query_place, key_place)).astype(jnp.bfloat16)
        residual = lax.dynamic_slice_in_dim(byte_states, offset, BYTE_DEV, 0)
        return (residual.astype(jnp.float32) + jnp.dot(mixed, w_out, preferred_element_type=jnp.float32)).astype(jnp.bfloat16)
    blocks = lax.map(one_block, jnp.arange(BYTES // BYTE_DEV, dtype=jnp.int32))
    return blocks.reshape(BYTES, DL)

def patch_block(encoded, flags, w_xq, w_xkv, w_up):
    patch_index = jnp.cumsum(flags) - 1
    patch_count = jnp.sum(flags)
    slot_list = jnp.arange(PATCH_CAP, dtype=jnp.int32)
    member = patch_index[None, :] == slot_list[:, None]
    live = slot_list < patch_count
    pooled = lax.optimization_barrier(jnp.max(jnp.where(member[:, :, None], encoded[None], jnp.asarray(very_negative, encoded.dtype)), axis=1))
    pooled = jnp.where(live[:, None], pooled, jnp.zeros_like(pooled))
    queries = jnp.dot(pooled, w_xq, preferred_element_type=jnp.float32).astype(jnp.bfloat16)
    pairs = jnp.dot(encoded, w_xkv, preferred_element_type=jnp.float32).astype(jnp.bfloat16)
    width_local = pairs.shape[1] // 2
    mixed = attend(heads_split(queries), heads_split(pairs[:, :width_local]), heads_split(pairs[:, width_local:]), member)
    patch_input = (pooled.astype(jnp.float32) + mixed).astype(jnp.bfloat16)
    state = jnp.dot(patch_input, w_up, preferred_element_type=jnp.float32)
    return jnp.where(live[:, None], state, jnp.zeros_like(state)).astype(jnp.bfloat16)

def decode_block(encoded, flags, states, dec_gain, w_dq, w_dkv, w_do):
    patch_index = jnp.cumsum(flags) - 1
    slot_list = jnp.arange(PATCH_CAP, dtype=jnp.int32)
    normed = rms_scale(encoded, dec_gain).astype(jnp.bfloat16)
    queries = jnp.dot(normed, w_dq, preferred_element_type=jnp.float32).astype(jnp.bfloat16)
    pairs = jnp.dot(states, w_dkv, preferred_element_type=jnp.float32).astype(jnp.bfloat16)
    width_local = pairs.shape[1] // 2
    allowed = slot_list[None, :] <= patch_index[:, None]
    mixed = attend(heads_split(queries), heads_split(pairs[:, :width_local]), heads_split(pairs[:, width_local:]), allowed).astype(jnp.bfloat16)
    return (encoded.astype(jnp.float32) + jnp.dot(mixed, w_do, preferred_element_type=jnp.float32)).astype(jnp.bfloat16)

def route_slots(expert_ids):
    flat = expert_ids.reshape(-1)
    onehot = (flat[:, None] == jnp.arange(EXPERTS, dtype=jnp.int32)[None, :]).astype(jnp.int32)
    ranked = jnp.cumsum(onehot, axis=0) - 1
    return lax.optimization_barrier(jnp.sum(ranked * onehot, axis=1)).reshape(expert_ids.shape)

def mixture(patch_state, expert_ids, moe_gain, w_router, w_in, w_down):
    devices = PATCHES // PATCH_CAP
    normed = rms_scale(patch_state, moe_gain).astype(jnp.bfloat16)
    logits = jnp.dot(normed.astype(jnp.float32), w_router, precision=lax.Precision.HIGHEST)
    gates = softmax_rows(jnp.take_along_axis(logits, expert_ids, axis=1))
    ids_blocks = expert_ids.reshape(devices, PATCH_CAP, 2)
    slot_number = jax.vmap(route_slots)(ids_blocks)
    target = ids_blocks * CAP + slot_number
    normed_blocks = normed.reshape(devices, PATCH_CAP, DG)

    def fill(rows, places):
        buffer = jnp.zeros((EXPERTS * CAP, DG), rows.dtype)
        return buffer.at[places[:, 0]].set(rows).at[places[:, 1]].set(rows)
    routed = jax.vmap(fill)(normed_blocks, target)
    routed = routed.reshape(devices, EXPERTS, CAP, DG).transpose(1, 0, 2, 3).reshape(EXPERTS, devices * CAP, DG)
    share = FF // N_SEQ

    def one_expert(packed):
        rows, paired, lowered = packed
        gate = jnp.dot(rows, paired[:, 0, :], preferred_element_type=jnp.float32)
        upper = jnp.dot(rows, paired[:, 1, :], preferred_element_type=jnp.float32)
        hidden = (jax.nn.silu(gate) * upper).astype(jnp.bfloat16)

        def add_block(block_index, total):
            offset = (jnp.asarray(block_index, jnp.int32) * share).astype(jnp.int32)
            part = lax.dynamic_slice_in_dim(hidden, offset, share, 1)
            weights_part = lax.dynamic_slice_in_dim(lowered, offset, share, 0)
            term = jnp.dot(part, weights_part, preferred_element_type=jnp.float32).astype(jnp.bfloat16)
            term = lax.optimization_barrier(term)
            return total + term.astype(jnp.float32)
        total = lax.fori_loop(0, N_SEQ, add_block, jnp.zeros((rows.shape[0], DG), jnp.float32))
        return total.astype(jnp.bfloat16)
    outputs = lax.map(one_expert, (routed, w_in, w_down))
    outputs = outputs.reshape(EXPERTS, devices, CAP, DG)
    device_index = jnp.arange(devices, dtype=jnp.int32)[:, None, None]
    chosen = outputs[ids_blocks, device_index, slot_number]
    gate_blocks = gates.reshape(devices, PATCH_CAP, 2)
    combined = lax.optimization_barrier(jnp.sum(gate_blocks[..., None] * chosen.astype(jnp.float32), axis=2))
    return (patch_state.astype(jnp.float32) + combined.reshape(PATCHES, DG)).astype(jnp.bfloat16)

def reference(byte_states, patch_start, expert_ids, enc_gain, w_qkv, w_out, w_xq, w_xkv, w_up, moe_gain, w_router, w_in, w_down, dec_gain, w_dq, w_dkv, w_do):
    devices = BYTES // BYTE_DEV
    encoded = encoder(byte_states, enc_gain, w_qkv, w_out)
    encoded_blocks = encoded.reshape(devices, BYTE_DEV, DL)
    flag_blocks = patch_start.reshape(devices, BYTE_DEV)
    states = lax.map(lambda packed: patch_block(packed[0], packed[1], w_xq, w_xkv, w_up), (encoded_blocks, flag_blocks))
    patch_state = states.reshape(PATCHES, DG)
    patch_out = mixture(patch_state, expert_ids, moe_gain, w_router, w_in, w_down)
    decoded = lax.map(lambda packed: decode_block(packed[0], packed[1], packed[2], dec_gain, w_dq, w_dkv, w_do), (encoded_blocks, flag_blocks, patch_out.reshape(devices, PATCH_CAP, DG)))
    return (decoded.reshape(BYTES, DL), patch_out)
```

```python
import math

import jax
import jax.numpy as jnp
from jax import lax
from jax.sharding import Mesh
from jax.sharding import PartitionSpec as P

HEADS_L = 8
HEAD = 64
WINDOW = 512
SEQ = ("seq_0", "seq_1")
SEQ_EXPERT = ("seq_0", "seq_1", "expert")


epsilon = 1e-06
very_negative = -1e30


def passed_along(x, axis, by):
    length = lax.axis_size(axis)
    pairs = [(i, i + by) for i in range(length) if 0 <= i + by < length]
    return lax.ppermute(x, axis, pairs)


def rms_scale(inputs, gain_vector):
    widened = inputs.astype(jnp.float32)
    return (
        widened
        * lax.rsqrt(jnp.mean(widened * widened, axis=-1, keepdims=True) + epsilon)
        * gain_vector
    )


def softmax_rows(scores):
    highest = jnp.max(scores, axis=-1, keepdims=True)
    raised = jnp.exp(scores - highest)
    return raised / jnp.sum(raised, axis=-1, keepdims=True)


def heads_split(inputs):
    return inputs.reshape(inputs.shape[0], HEADS_L, HEAD).transpose(1, 0, 2)


def heads_merge(inputs):
    return inputs.transpose(1, 0, 2).reshape(inputs.shape[1], HEADS_L * HEAD)


def attend(queries, keys, values, allowed):
    scores = jnp.einsum(
        "hqd,hkd->hqk", queries, keys, preferred_element_type=jnp.float32
    ) / math.sqrt(HEAD)
    scores = jnp.where(allowed[None], scores, very_negative)
    weights = softmax_rows(scores).astype(jnp.bfloat16)
    mixed = jnp.einsum("hqk,hkd->hqd", weights, values, preferred_element_type=jnp.float32)
    return heads_merge(mixed)


def window_mask(query_place, key_place):
    later = key_place[None, :]
    return (later >= 0) & (later <= query_place[:, None]) & (later > query_place[:, None] - WINDOW)


def patch_block(encoded, flags, w_xq, w_xkv, w_up):
    patch_cap = encoded.shape[0] * 5 // 32
    patch_index = jnp.cumsum(flags) - 1
    patch_count = jnp.sum(flags)
    slot_list = jnp.arange(patch_cap, dtype=jnp.int32)
    member = patch_index[None, :] == slot_list[:, None]
    live = slot_list < patch_count
    pooled = jnp.max(
        jnp.where(member[:, :, None], encoded[None], jnp.asarray(very_negative, encoded.dtype)),
        axis=1,
    )
    pooled = jnp.where(live[:, None], pooled, jnp.zeros_like(pooled))
    queries = jnp.dot(pooled, w_xq, preferred_element_type=jnp.float32).astype(jnp.bfloat16)
    pairs = jnp.dot(encoded, w_xkv, preferred_element_type=jnp.float32).astype(jnp.bfloat16)
    width_local = pairs.shape[1] // 2
    mixed = attend(
        heads_split(queries),
        heads_split(pairs[:, :width_local]),
        heads_split(pairs[:, width_local:]),
        member,
    )
    summed = pooled.astype(jnp.float32) + mixed
    patch_input = jnp.where(live[:, None], summed, 0.0).astype(jnp.bfloat16)
    state = jnp.dot(patch_input, w_up, preferred_element_type=jnp.float32).astype(jnp.bfloat16)
    return patch_input, state


def decode_block(encoded, flags, states, dec_gain, w_dq, w_dkv, w_do):
    patch_index = jnp.cumsum(flags) - 1
    slot_list = jnp.arange(states.shape[0], dtype=jnp.int32)
    normed = rms_scale(encoded, dec_gain).astype(jnp.bfloat16)
    queries = jnp.dot(normed, w_dq, preferred_element_type=jnp.float32).astype(jnp.bfloat16)
    pairs = jnp.dot(states, w_dkv, preferred_element_type=jnp.float32).astype(jnp.bfloat16)
    width_local = pairs.shape[1] // 2
    allowed = slot_list[None, :] <= patch_index[:, None]
    mixed = attend(
        heads_split(queries),
        heads_split(pairs[:, :width_local]),
        heads_split(pairs[:, width_local:]),
        allowed,
    ).astype(jnp.bfloat16)
    return (
        encoded.astype(jnp.float32) + jnp.dot(mixed, w_do, preferred_element_type=jnp.float32)
    ).astype(jnp.bfloat16)


def route_slots(expert_ids, experts):
    flat = expert_ids.reshape(-1)
    onehot = (flat[:, None] == jnp.arange(experts, dtype=jnp.int32)[None, :]).astype(jnp.int32)
    ranked = jnp.cumsum(onehot, axis=0) - 1
    return jnp.sum(ranked * onehot, axis=1).reshape(expert_ids.shape)


def folded_weights(w_up, moe_gain, w_in, w_down):
    scaled = (w_up.astype(jnp.float32) * moe_gain).astype(jnp.bfloat16)
    gate = lax.dot_general(w_in[0, :, 0, :], scaled, (((0,), (1,)), ((), ())), preferred_element_type=jnp.float32)
    upper = lax.dot_general(w_in[0, :, 1, :], scaled, (((0,), (1,)), ((), ())), preferred_element_type=jnp.float32)
    return jnp.concatenate(
        [gate.astype(jnp.bfloat16), upper.astype(jnp.bfloat16), w_down[0]], axis=1
    )


def mixture(patch_input, patch_state, expert_ids, moe_gain, w_router, weights):
    width = patch_input.shape[1]
    patch_cap = patch_state.shape[0]
    experts = w_router.shape[1]
    capacity = 12 * patch_cap // (5 * experts)
    widened = patch_state.astype(jnp.float32)
    scale = lax.rsqrt(jnp.mean(widened * widened, axis=-1, keepdims=True) + epsilon)
    normed = (widened * scale * moe_gain).astype(jnp.bfloat16)
    logits = jnp.dot(normed.astype(jnp.float32), w_router, precision=lax.Precision.HIGHEST)
    picked = expert_ids[:, :, None] == jnp.arange(experts, dtype=jnp.int32)[None, None, :]
    gates = softmax_rows(jnp.sum(jnp.where(picked, logits[:, None, :], 0.0), axis=2))
    slot_number = route_slots(expert_ids, experts)
    target = expert_ids * capacity + slot_number
    places = jnp.arange(experts * capacity, dtype=jnp.int32)
    chosen = target[None, :, :] == places[:, None, None]
    dispatch = jnp.sum(chosen.astype(jnp.bfloat16), axis=2)
    sent = (patch_input.astype(jnp.float32) * scale).astype(jnp.bfloat16)
    routed = jnp.dot(dispatch, sent, preferred_element_type=jnp.float32).astype(jnp.bfloat16)
    arrived = lax.all_to_all(
        routed.reshape(experts, capacity, width), "expert", split_axis=0, concat_axis=0, tiled=True
    )
    rows = lax.all_gather(
        arrived.reshape(experts * capacity, width), "seq_1", axis=0, tiled=True
    )
    over = (((1,), (1,)), ((), ()))
    gate = lax.dot_general(rows, weights[:, :width], over, preferred_element_type=jnp.float32)
    upper = lax.dot_general(
        rows, weights[:, width : 2 * width], over, preferred_element_type=jnp.float32
    )
    hidden = (jax.nn.silu(gate) * upper).astype(jnp.bfloat16)
    term = jnp.dot(hidden, weights[:, 2 * width :], preferred_element_type=jnp.float32).astype(
        jnp.bfloat16
    )
    summed = lax.psum_scatter(term, "seq_1", scatter_dimension=0, tiled=True)
    returned = lax.all_to_all(
        summed.reshape(experts, capacity, -1), "expert", split_axis=0, concat_axis=0, tiled=True
    ).reshape(experts * capacity, -1)
    weighted = jnp.sum(jnp.where(chosen, gates[None], 0.0), axis=2)
    high = weighted.astype(jnp.bfloat16)
    low = (weighted - high.astype(jnp.float32)).astype(jnp.bfloat16)
    rows_over = (((0,), (0,)), ((), ()))
    combined = lax.dot_general(
        high, returned, rows_over, preferred_element_type=jnp.float32
    ) + lax.dot_general(low, returned, rows_over, preferred_element_type=jnp.float32)
    return (widened + combined).astype(jnp.bfloat16)


def per_device(
    byte_states,
    patch_start,
    expert_ids,
    enc_gain,
    w_qkv,
    w_out,
    w_xq,
    w_xkv,
    w_up,
    moe_gain,
    w_router,
    w_in,
    w_down,
    dec_gain,
    w_dq,
    w_dkv,
    w_do,
):
    weights = lax.all_gather(
        folded_weights(w_up, moe_gain, w_in, w_down), "seq_0", axis=0, tiled=True
    )
    byte_dev = byte_states.shape[0]
    model_width = byte_states.shape[1]
    normed = rms_scale(byte_states, enc_gain).astype(jnp.bfloat16)
    projected = jnp.dot(normed, w_qkv, preferred_element_type=jnp.float32).astype(jnp.bfloat16)
    queries = projected[:, :model_width]
    own_pairs = projected[:, model_width:]
    reach = -(-WINDOW // byte_dev)
    earlier = []
    for distance in range(reach, 0, -1):
        moved = passed_along(normed, SEQ_EXPERT, distance)
        earlier.append(
            jnp.dot(moved, w_qkv[:, model_width:], preferred_element_type=jnp.float32).astype(
                jnp.bfloat16
            )
        )
    pairs = jnp.concatenate(earlier + [own_pairs], axis=0)
    offset = lax.axis_index(SEQ_EXPERT) * byte_dev
    query_place = offset + jnp.arange(byte_dev, dtype=jnp.int32)
    key_place = offset - reach * byte_dev + jnp.arange((reach + 1) * byte_dev, dtype=jnp.int32)
    mixed = attend(
        heads_split(queries),
        heads_split(pairs[:, :model_width]),
        heads_split(pairs[:, model_width:]),
        window_mask(query_place, key_place),
    ).astype(jnp.bfloat16)
    encoded = (
        byte_states.astype(jnp.float32) + jnp.dot(mixed, w_out, preferred_element_type=jnp.float32)
    ).astype(jnp.bfloat16)
    patch_input, patch_state = patch_block(encoded, patch_start, w_xq, w_xkv, w_up)
    patch_out = mixture(patch_input, patch_state, expert_ids, moe_gain, w_router, weights)
    bytes_out = decode_block(encoded, patch_start, patch_out, dec_gain, w_dq, w_dkv, w_do)
    return (bytes_out, patch_out)


def solution(mesh):
    split = Mesh(mesh.devices.reshape(4, 8, mesh.shape["expert"]), ("seq_0", "seq_1", "expert"))
    placed = (
        P(SEQ_EXPERT, None),
        P(SEQ_EXPERT),
        P(SEQ_EXPERT, None),
        P(),
        P(),
        P(),
        P(),
        P(),
        P(),
        P(),
        P(),
        P("expert", None, None, SEQ),
        P("expert", SEQ, None),
        P(),
        P(),
        P(),
        P(),
    )
    return jax.shard_map(
        per_device,
        mesh=split,
        in_specs=placed,
        out_specs=(P(SEQ_EXPERT, None), P(SEQ_EXPERT, None)),
        check_vma=False,
    )
```

```python
import functools
import math

import jax
import jax.numpy as jnp
from jax import lax
from jax.experimental import pallas as pl
from jax.experimental.pallas import tpu as pltpu
from jax.sharding import Mesh
from jax.sharding import PartitionSpec as P

HEADS_L = 8
HEAD = 64
WINDOW = 512
SEQ = ("seq_0", "seq_1")
SEQ_EXPERT = ("seq_0", "seq_1", "expert")


epsilon = 1e-06
very_negative = -1e30


def passed_along(x, axis, by):
    length = lax.axis_size(axis)
    pairs = [(i, i + by) for i in range(length) if 0 <= i + by < length]
    return lax.ppermute(x, axis, pairs)


def rms_scale(inputs, gain_vector):
    widened = inputs.astype(jnp.float32)
    return (
        widened
        * lax.rsqrt(jnp.mean(widened * widened, axis=-1, keepdims=True) + epsilon)
        * gain_vector
    )


def softmax_rows(scores):
    highest = jnp.max(scores, axis=-1, keepdims=True)
    raised = jnp.exp(scores - highest)
    return raised / jnp.sum(raised, axis=-1, keepdims=True)


def heads_split(inputs):
    return inputs.reshape(inputs.shape[0], HEADS_L, HEAD).transpose(1, 0, 2)


def heads_merge(inputs):
    return inputs.transpose(1, 0, 2).reshape(inputs.shape[1], HEADS_L * HEAD)


def attend(queries, keys, values, allowed):
    scores = jnp.einsum(
        "hqd,hkd->hqk", queries, keys, preferred_element_type=jnp.float32
    ) / math.sqrt(HEAD)
    scores = jnp.where(allowed[None], scores, very_negative)
    weights = softmax_rows(scores).astype(jnp.bfloat16)
    mixed = jnp.einsum("hqk,hkd->hqd", weights, values, preferred_element_type=jnp.float32)
    return heads_merge(mixed)


def window_mask(query_place, key_place):
    later = key_place[None, :]
    return (later >= 0) & (later <= query_place[:, None]) & (later > query_place[:, None] - WINDOW)


def patch_block(encoded, flags, w_xq, w_xkv, w_up):
    patch_cap = encoded.shape[0] * 5 // 32
    patch_index = jnp.cumsum(flags) - 1
    patch_count = jnp.sum(flags)
    slot_list = jnp.arange(patch_cap, dtype=jnp.int32)
    member = patch_index[None, :] == slot_list[:, None]
    live = slot_list < patch_count
    pooled = jnp.max(
        jnp.where(member[:, :, None], encoded[None], jnp.asarray(very_negative, encoded.dtype)),
        axis=1,
    )
    pooled = jnp.where(live[:, None], pooled, jnp.zeros_like(pooled))
    queries = jnp.dot(pooled, w_xq, preferred_element_type=jnp.float32).astype(jnp.bfloat16)
    pairs = jnp.dot(encoded, w_xkv, preferred_element_type=jnp.float32).astype(jnp.bfloat16)
    width_local = pairs.shape[1] // 2
    mixed = attend(
        heads_split(queries),
        heads_split(pairs[:, :width_local]),
        heads_split(pairs[:, width_local:]),
        member,
    )
    summed = pooled.astype(jnp.float32) + mixed
    patch_input = jnp.where(live[:, None], summed, 0.0).astype(jnp.bfloat16)
    state = jnp.dot(patch_input, w_up, preferred_element_type=jnp.float32).astype(jnp.bfloat16)
    return patch_input, state


def decode_block(encoded, flags, states, dec_gain, w_dq, w_dkv, w_do):
    patch_index = jnp.cumsum(flags) - 1
    slot_list = jnp.arange(states.shape[0], dtype=jnp.int32)
    normed = rms_scale(encoded, dec_gain).astype(jnp.bfloat16)
    queries = jnp.dot(normed, w_dq, preferred_element_type=jnp.float32).astype(jnp.bfloat16)
    pairs = jnp.dot(states, w_dkv, preferred_element_type=jnp.float32).astype(jnp.bfloat16)
    width_local = pairs.shape[1] // 2
    allowed = slot_list[None, :] <= patch_index[:, None]
    mixed = attend(
        heads_split(queries),
        heads_split(pairs[:, :width_local]),
        heads_split(pairs[:, width_local:]),
        allowed,
    ).astype(jnp.bfloat16)
    return (
        encoded.astype(jnp.float32) + jnp.dot(mixed, w_do, preferred_element_type=jnp.float32)
    ).astype(jnp.bfloat16)


def route_slots(expert_ids, experts):
    flat = expert_ids.reshape(-1)
    onehot = (flat[:, None] == jnp.arange(experts, dtype=jnp.int32)[None, :]).astype(jnp.int32)
    ranked = jnp.cumsum(onehot, axis=0) - 1
    return jnp.sum(ranked * onehot, axis=1).reshape(expert_ids.shape)


def folded_weights(w_up, moe_gain, w_in, w_down):
    scaled = (w_up.astype(jnp.float32) * moe_gain).astype(jnp.bfloat16)
    gate = lax.dot_general(w_in[0, :, 0, :], scaled, (((0,), (1,)), ((), ())), preferred_element_type=jnp.float32)
    upper = lax.dot_general(w_in[0, :, 1, :], scaled, (((0,), (1,)), ((), ())), preferred_element_type=jnp.float32)
    return jnp.concatenate(
        [gate.astype(jnp.bfloat16), upper.astype(jnp.bfloat16), w_down[0]], axis=1
    )


def exchange_kernel(
    ring,
    peers,
    routed,
    compact,
    spread,
    weights,
    out,
    held,
    landed,
    slots,
    hidden,
    sending,
    arriving,
    leaving,
    held_sem,
    out_send,
    out_recv,
    gather_send,
    gather_recv,
    ring_send,
    ring_recv,
    back_send,
    back_recv,
):
    mesh_id = pl.DeviceIdType.MESH
    at = lax.axis_index("seq_1")
    me = lax.axis_index("expert")
    right = {"seq_1": lax.rem(at + 1, ring)}
    left = {"seq_1": lax.rem(at + ring - 1, ring)}
    padded = routed.shape[0] // peers
    width = routed.shape[1]
    rows = compact.shape[0]
    share = sending.shape[3]
    half = ring // 2

    def peer(j):
        return {"expert": lax.rem(me + j, peers)}

    barrier = pltpu.get_barrier_semaphore()
    for device in [left, right] + [peer(j) for j in range(1, peers)]:
        pl.semaphore_signal(barrier, inc=1, device_id=device, device_id_type=mesh_id)
    fetch = pltpu.make_async_copy(weights, held, held_sem)
    fetch.start()
    pl.semaphore_wait(barrier, peers + 1)

    started = []

    def remote(source, target, send, recv, device):
        copy = pltpu.make_async_remote_copy(
            src_ref=source,
            dst_ref=target,
            send_sem=send,
            recv_sem=recv,
            device_id=device,
            device_id_type=mesh_id,
        )
        copy.start()
        started.append(copy)
        return copy

    outward = [
        remote(
            routed.at[pl.ds(j * padded, padded)],
            landed.at[pl.ds(j * padded, padded)],
            out_send.at[j],
            out_recv.at[j],
            peer(j),
        )
        for j in range(1, peers)
    ]
    landed[pl.ds(0, padded)] = routed[pl.ds(0, padded)]
    for copy in outward:
        copy.wait_recv()
    slots[0] = jnp.dot(
        compact[...], landed[...], preferred_element_type=jnp.float32
    ).astype(jnp.bfloat16)

    def forward_right(hop):
        if hop < half:
            source, target = slots.at[hop - 1], slots.at[hop]
        else:
            part = pl.ds(0, rows // 2)
            source, target = slots.at[hop - 1, part], slots.at[hop, part]
        return remote(source, target, gather_send.at[0, hop], gather_recv.at[0, hop], right)

    def forward_left(hop):
        begin, end = (ring - hop + 1) % ring, ring - hop
        if hop < half:
            source, target = slots.at[begin], slots.at[end]
        else:
            part = pl.ds(rows // 2, rows // 2)
            source, target = slots.at[begin, part], slots.at[end, part]
        return remote(source, target, gather_send.at[1, hop], gather_recv.at[1, hop], left)

    def fill_hidden(slot):
        over = (((1,), (1,)), ((), ()))
        block = slots[slot]
        gate = lax.dot_general(
            block, held[:, pl.ds(0, width)], over, preferred_element_type=jnp.float32
        )
        upper = lax.dot_general(
            block, held[:, pl.ds(width, width)], over, preferred_element_type=jnp.float32
        )
        hidden[slot] = (gate / (1.0 + jnp.exp(-gate)) * upper).astype(jnp.bfloat16)

    def term(slot, quarter):
        return jnp.dot(
            hidden[slot],
            held[:, pl.ds(2 * width + quarter * share, share)],
            preferred_element_type=jnp.float32,
        )

    to_right, to_left = forward_right(1), forward_left(1)
    fetch.wait()
    fill_hidden(0)
    rings = []
    for step in range(ring - 1):
        hop = step + 1
        if hop <= half:
            to_right.wait_recv()
            to_left.wait_recv()
            if hop < half:
                to_right, to_left = forward_right(hop + 1), forward_left(hop + 1)
            fill_hidden(hop)
            if hop < half:
                fill_hidden(ring - hop)
        current = []
        for quarter in (0, 2, 1, 3):
            total = term(hop if quarter < 2 else ring - hop, quarter)
            if step > 0:
                rings[quarter].wait_recv()
                total = total + arriving[quarter, step - 1].astype(jnp.float32)
            sending[quarter, step] = total.astype(jnp.bfloat16)
            current.append(
                remote(
                    sending.at[quarter, step],
                    arriving.at[quarter, step],
                    ring_send.at[quarter, step],
                    ring_recv.at[quarter, step],
                    right if quarter < 2 else left,
                )
            )
        rings = [current[0], current[2], current[1], current[3]]
    for quarter in (0, 2, 1, 3):
        total = term(0, quarter)
        rings[quarter].wait_recv()
        total = (total + arriving[quarter, ring - 2].astype(jnp.float32)).astype(jnp.bfloat16)
        leaving[:, pl.ds(quarter * share, share)] = jnp.dot(
            spread[...], total, preferred_element_type=jnp.float32
        ).astype(jnp.bfloat16)
    back = [
        remote(
            leaving.at[pl.ds(j * padded, padded)],
            out.at[pl.ds(j * padded, padded)],
            back_send.at[j],
            back_recv.at[j],
            {"expert": lax.rem(me + peers - j, peers)},
        )
        for j in range(1, peers)
    ]
    out[pl.ds(0, padded)] = leaving[pl.ds(0, padded)]
    for copy in back:
        copy.wait_recv()
    for copy in started:
        copy.wait_send()


def exchange(routed, weights, ring, peers, capacity):
    padded = routed.shape[0] // peers
    width = routed.shape[1]
    inner = weights.shape[0]
    outer = weights.shape[1] - 2 * width
    rows = peers * capacity
    share = outer // 4
    row = jnp.arange(rows)
    place = row // capacity * padded + row % capacity
    compact = (place[:, None] == jnp.arange(peers * padded)[None, :]).astype(jnp.bfloat16)
    dma = pltpu.SemaphoreType.DMA
    kept = jnp.bfloat16
    return pl.pallas_call(
        functools.partial(exchange_kernel, ring, peers),
        out_shape=jax.ShapeDtypeStruct((peers * padded, outer), kept),
        in_specs=[pl.BlockSpec(memory_space=pltpu.VMEM)] * 3
        + [pl.BlockSpec(memory_space=pl.ANY)],
        out_specs=pl.BlockSpec(memory_space=pltpu.VMEM),
        scratch_shapes=[
            pltpu.VMEM(weights.shape, kept),
            pltpu.VMEM(routed.shape, kept),
            pltpu.VMEM((ring, rows, width), kept),
            pltpu.VMEM((ring, rows, inner), kept),
            pltpu.VMEM((4, ring - 1, rows, share), kept),
            pltpu.VMEM((4, ring - 1, rows, share), kept),
            pltpu.VMEM((peers * padded, outer), kept),
            dma,
            dma((peers,)),
            dma((peers,)),
            dma((2, ring // 2 + 1)),
            dma((2, ring // 2 + 1)),
            dma((4, ring - 1)),
            dma((4, ring - 1)),
            dma((peers,)),
            dma((peers,)),
        ],
        compiler_params=pltpu.CompilerParams(
            collective_id=0, has_side_effects=True, vmem_limit_bytes=40 << 20
        ),
    )(routed, compact, compact.T, weights)


def mixture(patch_input, patch_state, expert_ids, moe_gain, w_router, weights):
    patch_cap = patch_state.shape[0]
    experts = w_router.shape[1]
    capacity = 12 * patch_cap // (5 * experts)
    padded = -(-capacity // 16) * 16
    widened = patch_state.astype(jnp.float32)
    scale = lax.rsqrt(jnp.mean(widened * widened, axis=-1, keepdims=True) + epsilon)
    normed = (widened * scale * moe_gain).astype(jnp.bfloat16)
    logits = jnp.dot(normed.astype(jnp.float32), w_router, precision=lax.Precision.HIGHEST)
    picked = expert_ids[:, :, None] == jnp.arange(experts, dtype=jnp.int32)[None, None, :]
    gates = softmax_rows(jnp.sum(jnp.where(picked, logits[:, None, :], 0.0), axis=2))
    slot_number = route_slots(expert_ids, experts)
    relative = lax.rem(expert_ids + experts - lax.axis_index("expert"), experts)
    target = relative * padded + slot_number
    places = jnp.arange(experts * padded, dtype=jnp.int32)
    chosen = target[None, :, :] == places[:, None, None]
    dispatch = jnp.sum(chosen.astype(jnp.bfloat16), axis=2)
    sent = (patch_input.astype(jnp.float32) * scale).astype(jnp.bfloat16)
    routed = jnp.dot(dispatch, sent, preferred_element_type=jnp.float32).astype(jnp.bfloat16)
    returned = exchange(routed, weights, lax.axis_size("seq_1"), experts, capacity)
    weighted = jnp.sum(jnp.where(chosen, gates[None], 0.0), axis=2)
    high = weighted.astype(jnp.bfloat16)
    low = (weighted - high.astype(jnp.float32)).astype(jnp.bfloat16)
    rows_over = (((0,), (0,)), ((), ()))
    combined = lax.dot_general(
        high, returned, rows_over, preferred_element_type=jnp.float32
    ) + lax.dot_general(low, returned, rows_over, preferred_element_type=jnp.float32)
    return (widened + combined).astype(jnp.bfloat16)


def per_device(
    byte_states,
    patch_start,
    expert_ids,
    enc_gain,
    w_qkv,
    w_out,
    w_xq,
    w_xkv,
    w_up,
    moe_gain,
    w_router,
    w_in,
    w_down,
    dec_gain,
    w_dq,
    w_dkv,
    w_do,
):
    weights = lax.all_gather(
        folded_weights(w_up, moe_gain, w_in, w_down), "seq_0", axis=0, tiled=True
    )
    byte_dev = byte_states.shape[0]
    model_width = byte_states.shape[1]
    normed = rms_scale(byte_states, enc_gain).astype(jnp.bfloat16)
    projected = jnp.dot(normed, w_qkv, preferred_element_type=jnp.float32).astype(jnp.bfloat16)
    queries = projected[:, :model_width]
    own_pairs = projected[:, model_width:]
    reach = -(-WINDOW // byte_dev)
    earlier = []
    for distance in range(reach, 0, -1):
        moved = passed_along(normed, SEQ_EXPERT, distance)
        earlier.append(
            jnp.dot(moved, w_qkv[:, model_width:], preferred_element_type=jnp.float32).astype(
                jnp.bfloat16
            )
        )
    pairs = jnp.concatenate(earlier + [own_pairs], axis=0)
    offset = lax.axis_index(SEQ_EXPERT) * byte_dev
    query_place = offset + jnp.arange(byte_dev, dtype=jnp.int32)
    key_place = offset - reach * byte_dev + jnp.arange((reach + 1) * byte_dev, dtype=jnp.int32)
    mixed = attend(
        heads_split(queries),
        heads_split(pairs[:, :model_width]),
        heads_split(pairs[:, model_width:]),
        window_mask(query_place, key_place),
    ).astype(jnp.bfloat16)
    encoded = (
        byte_states.astype(jnp.float32) + jnp.dot(mixed, w_out, preferred_element_type=jnp.float32)
    ).astype(jnp.bfloat16)
    patch_input, patch_state = patch_block(encoded, patch_start, w_xq, w_xkv, w_up)
    patch_out = mixture(patch_input, patch_state, expert_ids, moe_gain, w_router, weights)
    bytes_out = decode_block(encoded, patch_start, patch_out, dec_gain, w_dq, w_dkv, w_do)
    return (bytes_out, patch_out)


def solution(mesh):
    split = Mesh(mesh.devices.reshape(4, 8, mesh.shape["expert"]), ("seq_0", "seq_1", "expert"))
    placed = (
        P(SEQ_EXPERT, None),
        P(SEQ_EXPERT),
        P(SEQ_EXPERT, None),
        P(),
        P(),
        P(),
        P(),
        P(),
        P(),
        P(),
        P(),
        P("expert", None, None, SEQ),
        P("expert", SEQ, None),
        P(),
        P(),
        P(),
        P(),
    )
    return jax.shard_map(
        per_device,
        mesh=split,
        in_specs=placed,
        out_specs=(P(SEQ_EXPERT, None), P(SEQ_EXPERT, None)),
        check_vma=False,
    )
```

```python
import functools

import jax
import jax.numpy as jnp
from jax import lax
from jax.experimental import pallas as pl
from jax.experimental.pallas import tpu as pltpu
from jax.sharding import Mesh
from jax.sharding import PartitionSpec as P

HEADS = 8
HEAD = 64
PAIR = 2 * HEAD
PADDED = 16
LAG = 3
SEQ = ("seq_0", "seq_1")
SEQ_EXPERT = ("seq_0", "seq_1", "expert")

epsilon = 1e-06
very_negative = -1e30
bf16 = jnp.bfloat16
f32 = jnp.float32


def iota(shape, dimension):
    return lax.broadcasted_iota(jnp.int32, shape, dimension)


def mul(a, b):
    return jnp.dot(a, b, preferred_element_type=f32)


def mul_over_last(a, b):
    return lax.dot_general(a, b, (((1,), (1,)), ((), ())), preferred_element_type=f32)


def rms_scale(inputs, gain_vector):
    widened = inputs.astype(f32)
    return (
        widened
        * lax.rsqrt(jnp.mean(widened * widened, axis=-1, keepdims=True) + epsilon)
        * gain_vector
    )


def in_head(shape, h):
    lane = iota(shape, len(shape) - 1)
    return (lane >= h * HEAD) & (lane < (h + 1) * HEAD)


def step_kernel(
    sizes,
    states,
    flags,
    ids,
    enc_gain,
    moe_gain,
    dec_gain,
    w_router,
    folded,
    w_down,
    w_qkv_hbm,
    w_out_hbm,
    w_xq_hbm,
    w_xkv_hbm,
    w_up_hbm,
    w_dq_hbm,
    w_dkv_hbm,
    w_do_hbm,
    bytes_out,
    patch_out,
    w_qkv,
    w_out,
    w_xq,
    w_xkv,
    w_up,
    w_dq,
    w_dkv,
    w_do,
    up_held,
    down_held,
    halo,
    keys,
    values,
    mixing,
    routed,
    landed,
    slots,
    hidden,
    sending,
    arriving,
    leaving,
    returned,
    fetch_sem,
    halo_send,
    halo_recv,
    weight_send,
    weight_recv,
    out_send,
    out_recv,
    gather_send,
    gather_recv,
    ring_send,
    ring_recv,
    back_send,
    back_recv,
):
    groups, ring, peers = sizes
    mesh_id = pl.DeviceIdType.MESH
    plane = lax.axis_index("seq_0")
    at = lax.axis_index("seq_1")
    me = lax.axis_index("expert")
    right = {"seq_1": lax.rem(at + 1, ring)}
    left = {"seq_1": lax.rem(at + ring - 1, ring)}
    up = {"seq_0": lax.rem(plane + 1, groups)}
    down = {"seq_0": lax.rem(plane + groups - 1, groups)}
    count, width = states.shape
    slot_count, outer = patch_out.shape
    share = folded.shape[1]
    capacity = slots.shape[1] // peers
    rows = peers * capacity
    quarter_width = outer // 4
    half = ring // 2

    def peer(j):
        return {"expert": lax.rem(me + j, peers)}

    def stretch(by):
        moved = me + by + peers
        row = at + moved // peers - 1 + ring
        return {
            "seq_0": lax.rem(plane + row // ring - 1 + groups, groups),
            "seq_1": lax.rem(row, ring),
            "expert": lax.rem(moved, peers),
        }

    partners = [up, down, right, left] + [peer(j) for j in range(1, peers)]
    partners += [stretch(1), stretch(2), stretch(-1), stretch(-2)]
    barrier = pltpu.get_barrier_semaphore()
    for device in partners:
        pl.semaphore_signal(barrier, inc=1, device_id=device, device_id_type=mesh_id)

    fetches = {}
    for number, (name, source, target) in enumerate(
        [
            ("qkv", w_qkv_hbm, w_qkv),
            ("out", w_out_hbm, w_out),
            ("xkv", w_xkv_hbm, w_xkv),
            ("xq", w_xq_hbm, w_xq),
            ("w_up", w_up_hbm, w_up),
            ("up", folded, up_held.at[:, pl.ds(0, share)]),
            ("down", w_down, down_held.at[pl.ds(0, share)]),
            ("dq", w_dq_hbm, w_dq),
            ("dkv", w_dkv_hbm, w_dkv),
            ("do", w_do_hbm, w_do),
        ]
    ):
        fetches[name] = pltpu.make_async_copy(source, target, fetch_sem.at[number])
        fetches[name].start()
    pl.semaphore_wait(barrier, len(partners))

    started = []

    def remote(source, target, send, recv, device):
        copy = pltpu.make_async_remote_copy(
            src_ref=source,
            dst_ref=target,
            send_sem=send,
            recv_sem=recv,
            device_id=device,
            device_id_type=mesh_id,
        )
        copy.start()
        started.append(copy)
        return copy

    near = remote(states, halo.at[1], halo_send.at[0], halo_recv.at[0], stretch(1))
    far = remote(states, halo.at[0], halo_send.at[1], halo_recv.at[1], stretch(2))

    def weight_copy(stage, direction, source, target):
        return remote(
            source,
            target,
            weight_send.at[direction, stage],
            weight_recv.at[direction, stage],
            up if direction == 0 else down,
        )

    def up_slice(slot):
        return up_held.at[:, pl.ds(slot * share, share)]

    def down_slice(slot, part, rows_from=0, rows_count=None):
        return down_held.at[
            pl.ds(slot * share + rows_from, rows_count or share),
            pl.ds(part * (outer // 2), outer // 2),
        ]

    def pass_up_first():
        return [weight_copy(0, d, folded, up_slice((1, 3)[d])) for d in range(2)]

    def pass_up_second():
        copies = []
        for d in range(2):
            begin = up_held.at[d, pl.ds((1, 3)[d] * share, share)]
            copies.append(weight_copy(1, d, begin, up_held.at[d, pl.ds(2 * share, share)]))
        return copies

    def pass_down_first(part):
        source = w_down.at[:, pl.ds(part * (outer // 2), outer // 2)]
        return [
            weight_copy(2 + 2 * part, d, source, down_slice((1, 3)[d], part)) for d in range(2)
        ]

    def pass_down_second(part):
        return [
            weight_copy(
                3 + 2 * part,
                d,
                down_slice((1, 3)[d], part, d * (share // 2), share // 2),
                down_slice(2, part, d * (share // 2), share // 2),
            )
            for d in range(2)
        ]

    def landed_all(copies):
        for copy in copies:
            copy.wait_recv()

    up_first = pass_up_first()
    down_first = pass_down_first(0)

    def keep_pairs(number, projected):
        kept = projected.astype(bf16)
        keys[number] = kept[:, :width]
        values[number] = kept[:, width:]

    fetches["qkv"].wait()
    normed = rms_scale(states[...], enc_gain[...]).astype(bf16)
    queries = (mul(normed, w_qkv[:, pl.ds(0, width)]).astype(bf16).astype(f32) * 0.125).astype(bf16)
    keep_pairs(2, mul(normed, w_qkv[:, pl.ds(width, 2 * width)]))
    near.wait_recv()
    earlier = rms_scale(halo[1], enc_gain[...]).astype(bf16)
    keep_pairs(1, mul(earlier, w_qkv[:, pl.ds(width, 2 * width)]))
    far.wait_recv()
    earlier = rms_scale(halo[0], enc_gain[...]).astype(bf16)
    keep_pairs(0, mul(earlier, w_qkv[:, pl.ds(width, 2 * width)]))

    place = (plane * ring + at) * peers + me
    no_near = jnp.where(place < 1, very_negative, 0.0).astype(f32)
    no_far = jnp.where(place < 2, very_negative, 0.0).astype(f32)
    causal = iota((count, count), 1) <= iota((count, count), 0)
    first_half = iota((count, PAIR), 1) < HEAD
    for pair in range(HEADS // 2):
        columns = slice(pair * PAIR, (pair + 1) * PAIR)
        outs = []
        for side in range(2):
            asked = jnp.where(first_half == (side == 0), queries[:, columns].astype(f32), 0.0)
            asked = asked.astype(bf16)
            own = mul_over_last(asked, keys[2, :, columns])
            back_two = mul_over_last(asked, keys[0, :, columns]) + no_far
            back_one = mul_over_last(asked, keys[1, :, columns]) + no_near
            shared = jnp.where(causal, own, back_two)
            highest = jnp.maximum(
                jnp.max(shared, axis=-1, keepdims=True), jnp.max(back_one, axis=-1, keepdims=True)
            )
            shared = jnp.exp(shared - highest)
            back_one = jnp.exp(back_one - highest)
            total = jnp.sum(shared, axis=-1, keepdims=True) + jnp.sum(
                back_one, axis=-1, keepdims=True
            )
            mixed = (
                mul(jnp.where(causal, shared, 0.0).astype(bf16), values[2, :, columns])
                + mul(jnp.where(causal, 0.0, shared).astype(bf16), values[0, :, columns])
                + mul(back_one.astype(bf16), values[1, :, columns])
            )
            outs.append(mixed / total)
        mixing[:, columns] = jnp.where(first_half, outs[0], outs[1]).astype(bf16)
        if pair == 1:
            landed_all(up_first)
            up_second = pass_up_second()
    fetches["out"].wait()
    encoded = (states[...].astype(f32) + mul(mixing[...], w_out[...])).astype(bf16)

    opened = flags[...].astype(f32)
    row_at = iota((count, count), 0)
    column_at = iota((count, count), 1)
    opened_wide = jnp.broadcast_to(opened, (8, count)).astype(bf16)
    number_row = mul(opened_wide, (row_at <= column_at).astype(f32).astype(bf16))[:1] - 1.0
    next_row = mul(opened_wide, (row_at <= column_at + 1).astype(f32).astype(bf16))[:1] - 1.0
    last_row = (next_row > number_row) | (iota((1, count), 1) == count - 1)
    seen = (column_at <= row_at) & (opened > 0.5)
    number_column = jnp.sum(seen.astype(f32), axis=1, keepdims=True) - 1.0
    begin = jnp.max(jnp.where(seen, column_at, -1).astype(f32), axis=1, keepdims=True)
    depth = iota((count, 1), 0).astype(f32) - begin
    scanned = encoded.astype(f32)
    reach = 1
    while reach < count:
        moved = pltpu.roll(scanned, reach, 0)
        scanned = jnp.where(depth >= reach, jnp.maximum(scanned, moved), scanned)
        reach *= 2
    member = iota((slot_count, count), 0).astype(f32) == number_row
    live = jnp.max(member.astype(f32), axis=1, keepdims=True)
    chosen_last = jnp.where(member & last_row, 1.0, 0.0).astype(bf16)
    pooled = mul(chosen_last, scanned.astype(bf16))
    fetches["xkv"].wait()
    pairs = mul(encoded, w_xkv[...]).astype(bf16)
    fetches["xq"].wait()
    asked = mul(pooled.astype(bf16), w_xq[...]).astype(bf16).astype(f32) * 0.125
    stacked = jnp.concatenate(
        [jnp.where(in_head(asked.shape, h), asked, 0.0) for h in range(HEADS)], axis=0
    ).astype(bf16)
    bias = jnp.where(member, 0.0, very_negative)
    scores = mul_over_last(stacked, pairs[:, :width]) + jnp.concatenate([bias] * HEADS, axis=0)
    raised = jnp.exp(scores - jnp.max(scores, axis=-1, keepdims=True))
    weighed = (raised / jnp.sum(raised, axis=-1, keepdims=True)).astype(bf16)
    spread_out = mul(weighed, pairs[:, width:])
    patch_mix = pooled
    for h in range(HEADS):
        part = spread_out[h * slot_count : (h + 1) * slot_count]
        patch_mix = patch_mix + jnp.where(in_head(part.shape, h), part, 0.0)
    patch_input = jnp.where(live > 0.5, patch_mix, 0.0).astype(bf16)
    fetches["w_up"].wait()
    state = mul(patch_input, w_up[...]).astype(bf16).astype(f32)
    scale = lax.rsqrt(jnp.mean(state * state, axis=-1, keepdims=True) + epsilon)

    lane = iota((slot_count, peers * PADDED), 1)
    expert = [ids[:, k : k + 1] for k in range(2)]
    named = [jnp.where(lane == expert[k], 1.0, 0.0) for k in range(2)]
    before = jnp.where(iota((slot_count,) * 2, 1) < iota((slot_count,) * 2, 0), 1.0, 0.0)
    counted = mul(before.astype(bf16), (named[0] + named[1]).astype(bf16))
    target = []
    for k in range(2):
        rank = jnp.sum(counted * named[k], axis=1, keepdims=True).astype(jnp.int32)
        relative = expert[k] - me
        relative = jnp.where(relative < 0, relative + peers, relative)
        target.append(relative * PADDED + rank)
    placed = jnp.where((lane == target[0]) | (lane == target[1]), 1.0, 0.0)
    sent = (patch_input.astype(f32) * scale).astype(bf16)
    routed[...] = mul(jnp.transpose(placed).astype(bf16), sent).astype(bf16)

    outward = [
        remote(
            routed.at[pl.ds(j * PADDED, PADDED)],
            landed.at[pl.ds(j * PADDED, PADDED)],
            out_send.at[j],
            out_recv.at[j],
            peer(j),
        )
        for j in range(1, peers)
    ]
    landed[pl.ds(0, PADDED)] = routed[pl.ds(0, PADDED)]
    landed_all(down_first)
    down_second = pass_down_second(0)
    last_first = pass_down_first(1)

    patch_normed = (state * scale * moe_gain[...]).astype(bf16)
    logits = jnp.dot(
        patch_normed.astype(f32),
        w_router[...],
        precision=lax.Precision.HIGHEST,
        preferred_element_type=f32,
    )
    column = iota(logits.shape, 1)
    picked = [
        jnp.sum(jnp.where(column == expert[k], logits, 0.0), axis=1, keepdims=True)
        for k in range(2)
    ]
    top = jnp.maximum(picked[0], picked[1])
    raised = [jnp.exp(value - top) for value in picked]
    gates = [value / (raised[0] + raised[1]) for value in raised]
    weighted = jnp.where(lane == target[0], gates[0], 0.0) + jnp.where(
        lane == target[1], gates[1], 0.0
    )
    weighted_high = weighted.astype(bf16)
    weighted_low = (weighted - weighted_high.astype(f32)).astype(bf16)
    fetches["dq"].wait()
    byte_normed = rms_scale(encoded, dec_gain[...]).astype(bf16)
    byte_queries = (mul(byte_normed, w_dq[...]).astype(bf16).astype(f32) * 0.125).astype(bf16)

    def place_of(index):
        return (index >> 4) * capacity + (index & (PADDED - 1))

    def used(index):
        return (index & (PADDED - 1)) < capacity

    wide = iota((rows, peers * PADDED), 1)
    compact = jnp.where((iota(wide.shape, 0) == place_of(wide)) & used(wide), 1.0, 0.0)
    tall = iota((peers * PADDED, rows), 0)
    spread = jnp.where((iota(tall.shape, 1) == place_of(tall)) & used(tall), 1.0, 0.0)
    spread = spread.astype(bf16)

    landed_all(outward)
    slots[0] = mul(compact.astype(bf16), landed[...]).astype(bf16)

    def forward_right(hop):
        if hop < half:
            source, end = slots.at[hop - 1], slots.at[hop]
        else:
            part = pl.ds(0, rows // 2)
            source, end = slots.at[hop - 1, part], slots.at[hop, part]
        return remote(source, end, gather_send.at[0, hop], gather_recv.at[0, hop], right)

    def forward_left(hop):
        begin, finish = (ring - hop + 1) % ring, ring - hop
        if hop < half:
            source, end = slots.at[begin], slots.at[finish]
        else:
            part = pl.ds(rows // 2, rows // 2)
            source, end = slots.at[begin, part], slots.at[finish, part]
        return remote(source, end, gather_send.at[1, hop], gather_recv.at[1, hop], left)

    def fill_hidden(slot):
        block = slots[slot]
        gate = mul_over_last(block, up_held[0])
        upper = mul_over_last(block, up_held[1])
        hidden[slot] = (gate / (1.0 + jnp.exp(-gate)) * upper).astype(bf16)

    def term(slot, quarter):
        return mul(hidden[slot], down_held[:, pl.ds(quarter * quarter_width, quarter_width)])

    pending = [None] * 4

    def advance(quarter, step):
        total = term(step + 1 if quarter % 2 == 0 else ring - 1 - step, quarter)
        if step > 0:
            pending[quarter].wait_recv()
            total = total + arriving[quarter, step - 1].astype(f32)
        sending[quarter, step] = total.astype(bf16)
        pending[quarter] = remote(
            sending.at[quarter, step],
            arriving.at[quarter, step],
            ring_send.at[quarter, step],
            ring_recv.at[quarter, step],
            right if quarter % 2 == 0 else left,
        )

    to_right, to_left = forward_right(1), forward_left(1)
    fetches["up"].wait()
    landed_all(up_second)
    fill_hidden(0)
    for tick in range(ring - 1 + LAG):
        hop = tick + 1
        if hop <= half:
            landed_all([to_right, to_left])
            if hop < half:
                to_right, to_left = forward_right(hop + 1), forward_left(hop + 1)
            fill_hidden(hop)
            if hop < half:
                fill_hidden(ring - hop)
        if tick == 0:
            fetches["down"].wait()
            landed_all(down_second)
        if tick == max(LAG - 1, 0):
            landed_all(last_first)
            last_second = pass_down_second(1)
        if tick == LAG:
            landed_all(last_second)
        if tick < ring - 1:
            advance(0, tick)
            advance(1, tick)
        if tick >= LAG:
            advance(2, tick - LAG)
            advance(3, tick - LAG)
    for quarter in range(4):
        total = term(0, quarter)
        pending[quarter].wait_recv()
        total = (total + arriving[quarter, ring - 2].astype(f32)).astype(bf16)
        leaving[:, pl.ds(quarter * quarter_width, quarter_width)] = mul(spread, total).astype(bf16)
    back = [
        remote(
            leaving.at[pl.ds(j * PADDED, PADDED)],
            returned.at[pl.ds(j * PADDED, PADDED)],
            back_send.at[j],
            back_recv.at[j],
            peer(peers - j),
        )
        for j in range(1, peers)
    ]
    returned[pl.ds(0, PADDED)] = leaving[pl.ds(0, PADDED)]
    landed_all(back)

    combined = mul(weighted_high, returned[...]) + mul(weighted_low, returned[...])
    finished = (state + combined).astype(bf16)
    patch_out[...] = finished

    fetches["dkv"].wait()
    pairs = mul(finished, w_dkv[...]).astype(bf16).astype(f32)
    nothing = jnp.zeros((PAIR - slot_count, width), f32)

    def by_head(block):
        parts = []
        for h in range(HEADS):
            parts += [jnp.where(in_head(block.shape, h), block, 0.0), nothing]
        return jnp.concatenate(parts, axis=0).astype(bf16)

    scores = mul_over_last(byte_queries, by_head(pairs[:, :width]))
    allowed = iota((count, PAIR), 1).astype(f32) <= number_column
    weighed = []
    for h in range(HEADS):
        part = jnp.where(allowed, scores[:, h * PAIR : (h + 1) * PAIR], very_negative)
        raised = jnp.exp(part - jnp.max(part, axis=-1, keepdims=True))
        weighed.append((raised / jnp.sum(raised, axis=-1, keepdims=True)).astype(bf16))
    mixed = mul(jnp.concatenate(weighed, axis=1), by_head(pairs[:, width:])).astype(bf16)
    fetches["do"].wait()
    bytes_out[...] = (encoded.astype(f32) + mul(mixed, w_do[...])).astype(bf16)
    for copy in started:
        copy.wait_send()


def per_device(
    byte_states,
    patch_start,
    expert_ids,
    enc_gain,
    w_qkv,
    w_out,
    w_xq,
    w_xkv,
    w_up,
    moe_gain,
    w_router,
    w_in,
    w_down,
    dec_gain,
    w_dq,
    w_dkv,
    w_do,
):
    groups, ring, peers = (lax.axis_size(axis) for axis in SEQ_EXPERT)
    count, width = byte_states.shape
    slot_count = expert_ids.shape[0]
    outer = w_up.shape[1]
    share = w_down.shape[1]
    rows = peers * (12 * slot_count // (5 * peers))
    scaled = (w_up.astype(f32) * moe_gain).astype(bf16)
    folded = lax.dot_general(
        w_in[0], scaled, (((0,), (1,)), ((), ())), preferred_element_type=f32
    ).astype(bf16)
    dma = pltpu.SemaphoreType.DMA
    vmem = pltpu.VMEM
    weights = [w_qkv, w_out, w_xq, w_xkv, w_up, w_dq, w_dkv, w_do]
    return pl.pallas_call(
        functools.partial(step_kernel, (groups, ring, peers)),
        out_shape=(
            jax.ShapeDtypeStruct((count, width), bf16),
            jax.ShapeDtypeStruct((slot_count, outer), bf16),
        ),
        in_specs=[pl.BlockSpec(memory_space=pltpu.VMEM)] * 7
        + [pl.BlockSpec(memory_space=pl.ANY)] * 10,
        out_specs=(pl.BlockSpec(memory_space=pltpu.VMEM),) * 2,
        scratch_shapes=[vmem(w.shape, bf16) for w in weights]
        + [
            vmem((2, groups * share, width), bf16),
            vmem((groups * share, outer), bf16),
            vmem((2, count, width), bf16),
            vmem((3, count, width), bf16),
            vmem((3, count, width), bf16),
            vmem((count, width), bf16),
            vmem((peers * PADDED, width), bf16),
            vmem((peers * PADDED, width), bf16),
            vmem((ring, rows, width), bf16),
            vmem((ring, rows, groups * share), bf16),
            vmem((4, ring - 1, rows, outer // 4), bf16),
            vmem((4, ring - 1, rows, outer // 4), bf16),
            vmem((peers * PADDED, outer), bf16),
            vmem((peers * PADDED, outer), bf16),
            dma((10,)),
            dma((2,)),
            dma((2,)),
            dma((2, 6)),
            dma((2, 6)),
            dma((peers,)),
            dma((peers,)),
            dma((2, ring // 2 + 1)),
            dma((2, ring // 2 + 1)),
            dma((4, ring - 1)),
            dma((4, ring - 1)),
            dma((peers,)),
            dma((peers,)),
        ],
        compiler_params=pltpu.CompilerParams(
            collective_id=0, has_side_effects=True, vmem_limit_bytes=60 << 20
        ),
    )(
        byte_states,
        patch_start[None, :],
        expert_ids,
        enc_gain[None, :],
        moe_gain[None, :],
        dec_gain[None, :],
        w_router,
        folded,
        w_down[0],
        *weights,
    )


def solution(mesh):
    split = Mesh(mesh.devices.reshape(4, 8, mesh.shape["expert"]), SEQ_EXPERT)
    placed = (
        P(SEQ_EXPERT, None),
        P(SEQ_EXPERT),
        P(SEQ_EXPERT, None),
        P(),
        P(),
        P(),
        P(),
        P(),
        P(),
        P(),
        P(),
        P("expert", None, None, SEQ),
        P("expert", SEQ, None),
        P(),
        P(),
        P(),
        P(),
    )
    return jax.shard_map(
        per_device,
        mesh=split,
        in_specs=placed,
        out_specs=(P(SEQ_EXPERT, None), P(SEQ_EXPERT, None)),
        check_vma=False,
    )
```

```python
import functools

import jax
import jax.numpy as jnp
from jax import lax
from jax.experimental import pallas as pl
from jax.experimental.pallas import tpu as pltpu
from jax.sharding import Mesh
from jax.sharding import PartitionSpec as P

HEADS = 8
HEAD = 64
PAIR = 2 * HEAD
PADDED = 16
LAG = 3
SEQ = ("seq_0", "seq_1")
SEQ_EXPERT = ("seq_0", "seq_1", "expert")

epsilon = 1e-06
very_negative = -1e30
bf16 = jnp.bfloat16
f32 = jnp.float32


def iota(shape, dimension):
    return lax.broadcasted_iota(jnp.int32, shape, dimension)


def mul(a, b):
    return jnp.dot(a, b, preferred_element_type=f32)


def mul_over_last(a, b):
    return lax.dot_general(a, b, (((1,), (1,)), ((), ())), preferred_element_type=f32)


def rms_scale(inputs, gain_vector):
    widened = inputs.astype(f32)
    return (
        widened
        * lax.rsqrt(jnp.mean(widened * widened, axis=-1, keepdims=True) + epsilon)
        * gain_vector
    )


def in_head(shape, h):
    lane = iota(shape, len(shape) - 1)
    return (lane >= h * HEAD) & (lane < (h + 1) * HEAD)


def step_kernel(
    sizes,
    states_hbm,
    flags_hbm,
    ids_hbm,
    enc_gain_hbm,
    moe_gain_hbm,
    dec_gain_hbm,
    w_router_hbm,
    w_in_hbm,
    w_down,
    w_qkv_hbm,
    w_out_hbm,
    w_xq_hbm,
    w_xkv_hbm,
    w_up_hbm,
    w_dq_hbm,
    w_dkv_hbm,
    w_do_hbm,
    bytes_out,
    patch_out,
    states,
    flags,
    ids,
    enc_gain,
    moe_gain,
    dec_gain,
    w_router,
    w_in,
    w_qkv,
    w_out,
    w_xq,
    w_xkv,
    w_up,
    w_dq,
    w_dkv,
    w_do,
    up_held,
    down_held,
    halo,
    keys,
    values,
    mixing,
    routed,
    landed,
    slots,
    hidden,
    sending,
    arriving,
    leaving,
    returned,
    fetch_sem,
    halo_send,
    halo_recv,
    weight_send,
    weight_recv,
    out_send,
    out_recv,
    gather_send,
    gather_recv,
    ring_send,
    ring_recv,
    back_send,
    back_recv,
):
    groups, ring, peers = sizes
    mesh_id = pl.DeviceIdType.MESH
    plane = lax.axis_index("seq_0")
    at = lax.axis_index("seq_1")
    me = lax.axis_index("expert")
    right = {"seq_1": lax.rem(at + 1, ring)}
    left = {"seq_1": lax.rem(at + ring - 1, ring)}
    up = {"seq_0": lax.rem(plane + 1, groups)}
    down = {"seq_0": lax.rem(plane + groups - 1, groups)}
    count, width = states.shape
    slot_count, outer = patch_out.shape
    share = w_down.shape[0]
    capacity = slots.shape[1] // peers
    rows = peers * capacity
    quarter_width = outer // 4
    half = ring // 2

    def peer(j):
        return {"expert": lax.rem(me + j, peers)}

    def stretch(by):
        moved = me + by + peers
        row = at + moved // peers - 1 + ring
        return {
            "seq_0": lax.rem(plane + row // ring - 1 + groups, groups),
            "seq_1": lax.rem(row, ring),
            "expert": lax.rem(moved, peers),
        }

    partners = [up, down, right, left] + [peer(j) for j in range(1, peers)]
    partners += [stretch(1), stretch(2), stretch(-1), stretch(-2)]
    barrier = pltpu.get_barrier_semaphore()
    for device in partners:
        pl.semaphore_signal(barrier, inc=1, device_id=device, device_id_type=mesh_id)

    fetches = {}
    for number, (name, source, target) in enumerate(
        [
            ("states", states_hbm, states),
            ("moe_gain", moe_gain_hbm, moe_gain),
            ("w_in", w_in_hbm, w_in),
            ("w_up", w_up_hbm, w_up),
            ("enc_gain", enc_gain_hbm, enc_gain),
            ("qkv", w_qkv_hbm, w_qkv),
            ("flags", flags_hbm, flags),
            ("ids", ids_hbm, ids),
            ("out", w_out_hbm, w_out),
            ("xkv", w_xkv_hbm, w_xkv),
            ("xq", w_xq_hbm, w_xq),
            ("router", w_router_hbm, w_router),
            ("dec_gain", dec_gain_hbm, dec_gain),
            ("down", w_down, down_held.at[pl.ds(0, share)]),
            ("dq", w_dq_hbm, w_dq),
            ("dkv", w_dkv_hbm, w_dkv),
            ("do", w_do_hbm, w_do),
        ]
    ):
        fetches[name] = pltpu.make_async_copy(source, target, fetch_sem.at[number])
    late = ("down", "dq", "dkv", "do")
    for name in fetches:
        if name not in late:
            fetches[name].start()
    pl.semaphore_wait(barrier, len(partners))

    started = []

    def remote(source, target, send, recv, device):
        copy = pltpu.make_async_remote_copy(
            src_ref=source,
            dst_ref=target,
            send_sem=send,
            recv_sem=recv,
            device_id=device,
            device_id_type=mesh_id,
        )
        copy.start()
        started.append(copy)
        return copy

    near = remote(states_hbm, halo.at[1], halo_send.at[0], halo_recv.at[0], stretch(1))
    far = remote(states_hbm, halo.at[0], halo_send.at[1], halo_recv.at[1], stretch(2))

    def weight_copy(stage, direction, source, target):
        return remote(
            source,
            target,
            weight_send.at[direction, stage],
            weight_recv.at[direction, stage],
            up if direction == 0 else down,
        )

    def up_slice(slot):
        return up_held.at[:, pl.ds(slot * share, share)]

    def down_slice(slot, part, rows_from=0, rows_count=None):
        return down_held.at[
            pl.ds(slot * share + rows_from, rows_count or share),
            pl.ds(part * (outer // 2), outer // 2),
        ]

    def pass_up_first():
        return [weight_copy(0, d, up_slice(0), up_slice((1, 3)[d])) for d in range(2)]

    def pass_up_second():
        copies = []
        for d in range(2):
            begin = up_held.at[d, pl.ds((1, 3)[d] * share, share)]
            copies.append(weight_copy(1, d, begin, up_held.at[d, pl.ds(2 * share, share)]))
        return copies

    def pass_down_first(part):
        source = w_down.at[:, pl.ds(part * (outer // 2), outer // 2)]
        return [
            weight_copy(2 + 2 * part, d, source, down_slice((1, 3)[d], part)) for d in range(2)
        ]

    def pass_down_second(part):
        return [
            weight_copy(
                3 + 2 * part,
                d,
                down_slice((1, 3)[d], part, d * (share // 2), share // 2),
                down_slice(2, part, d * (share // 2), share // 2),
            )
            for d in range(2)
        ]

    def landed_all(copies):
        for copy in copies:
            copy.wait_recv()

    down_first = pass_down_first(0)
    for name in ("moe_gain", "w_in", "w_up"):
        fetches[name].wait()
    scaled = (w_in[...].astype(f32) * moe_gain[...]).astype(bf16)
    folded = mul_over_last(scaled, w_up[...]).astype(bf16)
    up_held[0, pl.ds(0, share)] = folded[:share]
    up_held[1, pl.ds(0, share)] = folded[share:]
    up_first = pass_up_first()

    def keep_pairs(number, projected):
        kept = projected.astype(bf16)
        keys[number] = kept[:, :width]
        values[number] = kept[:, width:]

    for name in ("states", "enc_gain", "qkv"):
        fetches[name].wait()
    normed = rms_scale(states[...], enc_gain[...]).astype(bf16)
    queries = (mul(normed, w_qkv[:, pl.ds(0, width)]).astype(bf16).astype(f32) * 0.125).astype(bf16)
    keep_pairs(2, mul(normed, w_qkv[:, pl.ds(width, 2 * width)]))
    near.wait_recv()
    earlier = rms_scale(halo[1], enc_gain[...]).astype(bf16)
    keep_pairs(1, mul(earlier, w_qkv[:, pl.ds(width, 2 * width)]))
    far.wait_recv()
    earlier = rms_scale(halo[0], enc_gain[...]).astype(bf16)
    keep_pairs(0, mul(earlier, w_qkv[:, pl.ds(width, 2 * width)]))

    place = (plane * ring + at) * peers + me
    no_near = jnp.where(place < 1, very_negative, 0.0).astype(f32)
    no_far = jnp.where(place < 2, very_negative, 0.0).astype(f32)
    causal = iota((count, count), 1) <= iota((count, count), 0)
    first_half = iota((count, PAIR), 1) < HEAD
    for pair in range(HEADS // 2):
        columns = slice(pair * PAIR, (pair + 1) * PAIR)
        outs = []
        for side in range(2):
            asked = jnp.where(first_half == (side == 0), queries[:, columns].astype(f32), 0.0)
            asked = asked.astype(bf16)
            own = mul_over_last(asked, keys[2, :, columns])
            back_two = mul_over_last(asked, keys[0, :, columns]) + no_far
            back_one = mul_over_last(asked, keys[1, :, columns]) + no_near
            shared = jnp.where(causal, own, back_two)
            highest = jnp.maximum(
                jnp.max(shared, axis=-1, keepdims=True), jnp.max(back_one, axis=-1, keepdims=True)
            )
            shared = jnp.exp(shared - highest)
            back_one = jnp.exp(back_one - highest)
            total = jnp.sum(shared, axis=-1, keepdims=True) + jnp.sum(
                back_one, axis=-1, keepdims=True
            )
            mixed = (
                mul(jnp.where(causal, shared, 0.0).astype(bf16), values[2, :, columns])
                + mul(jnp.where(causal, 0.0, shared).astype(bf16), values[0, :, columns])
                + mul(back_one.astype(bf16), values[1, :, columns])
            )
            outs.append(mixed / total)
        mixing[:, columns] = jnp.where(first_half, outs[0], outs[1]).astype(bf16)
        if pair == 1:
            landed_all(down_first)
            down_second = pass_down_second(0)
    fetches["out"].wait()
    for name in late:
        fetches[name].start()
    encoded = (states[...].astype(f32) + mul(mixing[...], w_out[...])).astype(bf16)

    fetches["flags"].wait()
    opened = flags[...].astype(f32)
    row_at = iota((count, count), 0)
    column_at = iota((count, count), 1)
    opened_wide = jnp.broadcast_to(opened, (8, count)).astype(bf16)
    number_row = mul(opened_wide, (row_at <= column_at).astype(f32).astype(bf16))[:1] - 1.0
    next_row = mul(opened_wide, (row_at <= column_at + 1).astype(f32).astype(bf16))[:1] - 1.0
    last_row = (next_row > number_row) | (iota((1, count), 1) == count - 1)
    seen = (column_at <= row_at) & (opened > 0.5)
    number_column = jnp.sum(seen.astype(f32), axis=1, keepdims=True) - 1.0
    begin = jnp.max(jnp.where(seen, column_at, -1).astype(f32), axis=1, keepdims=True)
    depth = iota((count, 1), 0).astype(f32) - begin
    scanned = encoded.astype(f32)
    reach = 1
    while reach < count:
        moved = pltpu.roll(scanned, reach, 0)
        scanned = jnp.where(depth >= reach, jnp.maximum(scanned, moved), scanned)
        reach *= 2
    member = iota((slot_count, count), 0).astype(f32) == number_row
    live = jnp.max(member.astype(f32), axis=1, keepdims=True)
    chosen_last = jnp.where(member & last_row, 1.0, 0.0).astype(bf16)
    pooled = mul(chosen_last, scanned.astype(bf16))
    fetches["xkv"].wait()
    pairs = mul(encoded, w_xkv[...]).astype(bf16)
    fetches["xq"].wait()
    asked = mul(pooled.astype(bf16), w_xq[...]).astype(bf16).astype(f32) * 0.125
    stacked = jnp.concatenate(
        [jnp.where(in_head(asked.shape, h), asked, 0.0) for h in range(HEADS)], axis=0
    ).astype(bf16)
    bias = jnp.where(member, 0.0, very_negative)
    scores = mul_over_last(stacked, pairs[:, :width]) + jnp.concatenate([bias] * HEADS, axis=0)
    raised = jnp.exp(scores - jnp.max(scores, axis=-1, keepdims=True))
    weighed = (raised / jnp.sum(raised, axis=-1, keepdims=True)).astype(bf16)
    spread_out = mul(weighed, pairs[:, width:])
    patch_mix = pooled
    for h in range(HEADS):
        part = spread_out[h * slot_count : (h + 1) * slot_count]
        patch_mix = patch_mix + jnp.where(in_head(part.shape, h), part, 0.0)
    patch_input = jnp.where(live > 0.5, patch_mix, 0.0).astype(bf16)
    state = mul(patch_input, w_up[...]).astype(bf16).astype(f32)
    scale = lax.rsqrt(jnp.mean(state * state, axis=-1, keepdims=True) + epsilon)

    lane = iota((slot_count, peers * PADDED), 1)
    fetches["ids"].wait()
    same = iota((slot_count,) * 2, 0) == iota((slot_count,) * 2, 1)
    ids_row = [ids[k : k + 1].astype(f32) for k in range(2)]
    expert = [
        jnp.sum(jnp.where(same, row, 0.0), axis=1, keepdims=True).astype(jnp.int32)
        for row in ids_row
    ]
    named = [jnp.where(lane == expert[k], 1.0, 0.0) for k in range(2)]
    before = jnp.where(iota((slot_count,) * 2, 1) < iota((slot_count,) * 2, 0), 1.0, 0.0)
    counted = mul(before.astype(bf16), (named[0] + named[1]).astype(bf16))
    target = []
    for k in range(2):
        rank = jnp.sum(counted * named[k], axis=1, keepdims=True).astype(jnp.int32)
        relative = expert[k] - me
        relative = jnp.where(relative < 0, relative + peers, relative)
        target.append(relative * PADDED + rank)
    placed = jnp.where((lane == target[0]) | (lane == target[1]), 1.0, 0.0)
    sent = (patch_input.astype(f32) * scale).astype(bf16)
    routed[...] = mul(jnp.transpose(placed).astype(bf16), sent).astype(bf16)

    outward = [
        remote(
            routed.at[pl.ds(j * PADDED, PADDED)],
            landed.at[pl.ds(j * PADDED, PADDED)],
            out_send.at[j],
            out_recv.at[j],
            peer(j),
        )
        for j in range(1, peers)
    ]
    landed[pl.ds(0, PADDED)] = routed[pl.ds(0, PADDED)]

    patch_normed = (state * scale * moe_gain[...]).astype(bf16)
    fetches["router"].wait()
    logits = lax.dot_general(
        patch_normed.astype(f32),
        w_router[...],
        (((1,), (1,)), ((), ())),
        precision=lax.Precision.HIGHEST,
        preferred_element_type=f32,
    )
    column = iota(logits.shape, 1)
    picked = [
        jnp.sum(jnp.where(column == expert[k], logits, 0.0), axis=1, keepdims=True)
        for k in range(2)
    ]
    top = jnp.maximum(picked[0], picked[1])
    raised = [jnp.exp(value - top) for value in picked]
    gates = [value / (raised[0] + raised[1]) for value in raised]
    weighted = jnp.where(lane == target[0], gates[0], 0.0) + jnp.where(
        lane == target[1], gates[1], 0.0
    )
    weighted_high = weighted.astype(bf16)
    weighted_low = (weighted - weighted_high.astype(f32)).astype(bf16)
    fetches["dq"].wait()
    fetches["dec_gain"].wait()
    byte_normed = rms_scale(encoded, dec_gain[...]).astype(bf16)
    byte_queries = (mul(byte_normed, w_dq[...]).astype(bf16).astype(f32) * 0.125).astype(bf16)

    def place_of(index):
        return (index >> 4) * capacity + (index & (PADDED - 1))

    def used(index):
        return (index & (PADDED - 1)) < capacity

    wide = iota((rows, peers * PADDED), 1)
    compact = jnp.where((iota(wide.shape, 0) == place_of(wide)) & used(wide), 1.0, 0.0)
    tall = iota((peers * PADDED, rows), 0)
    spread = jnp.where((iota(tall.shape, 1) == place_of(tall)) & used(tall), 1.0, 0.0)
    spread = spread.astype(bf16)

    landed_all(outward)
    slots[0] = mul(compact.astype(bf16), landed[...]).astype(bf16)

    def forward_right(hop):
        if hop < half:
            source, end = slots.at[hop - 1], slots.at[hop]
        else:
            part = pl.ds(0, rows // 2)
            source, end = slots.at[hop - 1, part], slots.at[hop, part]
        return remote(source, end, gather_send.at[0, hop], gather_recv.at[0, hop], right)

    def forward_left(hop):
        begin, finish = (ring - hop + 1) % ring, ring - hop
        if hop < half:
            source, end = slots.at[begin], slots.at[finish]
        else:
            part = pl.ds(rows // 2, rows // 2)
            source, end = slots.at[begin, part], slots.at[finish, part]
        return remote(source, end, gather_send.at[1, hop], gather_recv.at[1, hop], left)

    def fill_hidden(slot):
        block = slots[slot]
        gate = mul_over_last(block, up_held[0])
        upper = mul_over_last(block, up_held[1])
        hidden[slot] = (gate / (1.0 + jnp.exp(-gate)) * upper).astype(bf16)

    def term(slot, quarter):
        return mul(hidden[slot], down_held[:, pl.ds(quarter * quarter_width, quarter_width)])

    pending = [None] * 4

    def advance(quarter, step):
        total = term(step + 1 if quarter % 2 == 0 else ring - 1 - step, quarter)
        if step > 0:
            pending[quarter].wait_recv()
            total = total + arriving[quarter, step - 1].astype(f32)
        sending[quarter, step] = total.astype(bf16)
        pending[quarter] = remote(
            sending.at[quarter, step],
            arriving.at[quarter, step],
            ring_send.at[quarter, step],
            ring_recv.at[quarter, step],
            right if quarter % 2 == 0 else left,
        )

    def send_back(part):
        columns = pl.ds(part * (outer // 2), outer // 2)
        for quarter in (2 * part, 2 * part + 1):
            total = term(0, quarter)
            pending[quarter].wait_recv()
            total = (total + arriving[quarter, ring - 2].astype(f32)).astype(bf16)
            leaving[:, pl.ds(quarter * quarter_width, quarter_width)] = mul(
                spread, total
            ).astype(bf16)
        copies = []
        for j in range(1, peers):
            rows_of = pl.ds(j * PADDED, PADDED)
            copies.append(
                remote(
                    leaving.at[rows_of, columns],
                    returned.at[rows_of, columns],
                    back_send.at[part, j],
                    back_recv.at[part, j],
                    peer(peers - j),
                )
            )
        returned[pl.ds(0, PADDED), columns] = leaving[pl.ds(0, PADDED), columns]
        return copies

    to_right, to_left = forward_right(1), forward_left(1)
    landed_all(up_first)
    up_second = pass_up_second()
    last_first = pass_down_first(1)
    landed_all(up_second)
    fill_hidden(0)
    for tick in range(ring - 1 + LAG):
        hop = tick + 1
        if hop <= half:
            landed_all([to_right, to_left])
            if hop < half:
                to_right, to_left = forward_right(hop + 1), forward_left(hop + 1)
            fill_hidden(hop)
            if hop < half:
                fill_hidden(ring - hop)
        if tick == 0:
            fetches["down"].wait()
            landed_all(down_second)
        if tick == max(LAG - 1, 0):
            landed_all(last_first)
            last_second = pass_down_second(1)
        if tick == LAG:
            landed_all(last_second)
        if tick < ring - 1:
            advance(0, tick)
            advance(1, tick)
        if tick >= LAG:
            advance(2, tick - LAG)
            advance(3, tick - LAG)
        if tick == ring - 1:
            back = [send_back(0)]
    if LAG == 0:
        back = [send_back(0)]
    back.append(send_back(1))

    fetches["dkv"].wait()
    pairs = 0.0
    for part in range(2):
        columns = pl.ds(part * (outer // 2), outer // 2)
        landed_all(back[part])
        combined = mul(weighted_high, returned[:, columns]) + mul(
            weighted_low, returned[:, columns]
        )
        finished = state[:, part * (outer // 2) : (part + 1) * (outer // 2)] + combined
        patch_out[:, columns] = finished
        pairs = pairs + mul(finished.astype(bf16), w_dkv[columns])

    pairs = pairs.astype(bf16).astype(f32)
    nothing = jnp.zeros((PAIR - slot_count, width), f32)

    def by_head(block):
        parts = []
        for h in range(HEADS):
            parts += [jnp.where(in_head(block.shape, h), block, 0.0), nothing]
        return jnp.concatenate(parts, axis=0).astype(bf16)

    scores = mul_over_last(byte_queries, by_head(pairs[:, :width]))
    allowed = iota((count, PAIR), 1).astype(f32) <= number_column
    weighed = []
    for h in range(HEADS):
        part = jnp.where(allowed, scores[:, h * PAIR : (h + 1) * PAIR], very_negative)
        raised = jnp.exp(part - jnp.max(part, axis=-1, keepdims=True))
        weighed.append((raised / jnp.sum(raised, axis=-1, keepdims=True)).astype(bf16))
    mixed = mul(jnp.concatenate(weighed, axis=1), by_head(pairs[:, width:])).astype(bf16)
    fetches["do"].wait()
    bytes_out[...] = encoded.astype(f32) + mul(mixed, w_do[...])
    for copy in started:
        copy.wait_send()


def per_device(
    byte_states,
    patch_start,
    expert_ids,
    enc_gain,
    w_qkv,
    w_out,
    w_xq,
    w_xkv,
    w_up,
    moe_gain,
    w_router,
    w_in,
    w_down,
    dec_gain,
    w_dq,
    w_dkv,
    w_do,
):
    groups, ring, peers = (lax.axis_size(axis) for axis in SEQ_EXPERT)
    count, width = byte_states.shape
    slot_count = expert_ids.shape[0]
    outer = w_up.shape[1]
    share = w_down.shape[1]
    rows = peers * (12 * slot_count // (5 * peers))
    dma = pltpu.SemaphoreType.DMA
    vmem = pltpu.VMEM
    small = [
        byte_states,
        patch_start[None, :],
        expert_ids.T,
        enc_gain[None, :],
        moe_gain[None, :],
        dec_gain[None, :],
        w_router.T,
        jnp.transpose(w_in[0], (1, 2, 0)).reshape(2 * share, outer),
    ]
    weights = [w_qkv, w_out, w_xq, w_xkv, w_up, w_dq, w_dkv, w_do]
    made = pl.pallas_call(
        functools.partial(step_kernel, (groups, ring, peers)),
        out_shape=(
            jax.ShapeDtypeStruct((count, width), f32),
            jax.ShapeDtypeStruct((slot_count, outer), f32),
        ),
        in_specs=[pl.BlockSpec(memory_space=pl.ANY)] * 17,
        out_specs=(pl.BlockSpec(memory_space=pltpu.VMEM),) * 2,
        scratch_shapes=[vmem(w.shape, w.dtype) for w in small + weights]
        + [
            vmem((2, groups * share, width), bf16),
            vmem((groups * share, outer), bf16),
            vmem((2, count, width), bf16),
            vmem((3, count, width), bf16),
            vmem((3, count, width), bf16),
            vmem((count, width), bf16),
            vmem((peers * PADDED, width), bf16),
            vmem((peers * PADDED, width), bf16),
            vmem((ring, rows, width), bf16),
            vmem((ring, rows, groups * share), bf16),
            vmem((4, ring - 1, rows, outer // 4), bf16),
            vmem((4, ring - 1, rows, outer // 4), bf16),
            vmem((peers * PADDED, outer), bf16),
            vmem((peers * PADDED, outer), bf16),
            dma((17,)),
            dma((2,)),
            dma((2,)),
            dma((2, 6)),
            dma((2, 6)),
            dma((peers,)),
            dma((peers,)),
            dma((2, ring // 2 + 1)),
            dma((2, ring // 2 + 1)),
            dma((4, ring - 1)),
            dma((4, ring - 1)),
            dma((2, peers)),
            dma((2, peers)),
        ],
        compiler_params=pltpu.CompilerParams(
            collective_id=0, has_side_effects=True, vmem_limit_bytes=64000000
        ),
    )(*small, w_down[0], *weights)
    return tuple(value.astype(bf16) for value in made)


def solution(mesh):
    split = Mesh(mesh.devices.reshape(4, 8, mesh.shape["expert"]), SEQ_EXPERT)
    placed = (
        P(SEQ_EXPERT, None),
        P(SEQ_EXPERT),
        P(SEQ_EXPERT, None),
        P(),
        P(),
        P(),
        P(),
        P(),
        P(),
        P(),
        P(),
        P("expert", None, None, SEQ),
        P("expert", SEQ, None),
        P(),
        P(),
        P(),
        P(),
    )
    return jax.shard_map(
        per_device,
        mesh=split,
        in_specs=placed,
        out_specs=(P(SEQ_EXPERT, None), P(SEQ_EXPERT, None)),
        check_vma=False,
    )
```

```python
import functools

import jax
import jax.numpy as jnp
from jax import lax
from jax.experimental import pallas as pl
from jax.experimental.pallas import tpu as pltpu
from jax.sharding import Mesh
from jax.sharding import PartitionSpec as P

HEADS = 8
HEAD = 64
PAIR = 2 * HEAD
PADDED = 16
PARTS = (1024, 1024)
LAGS = (0, 2)
PIECES = 2
SEQ = ("seq_0", "seq_1")
SEQ_EXPERT = ("seq_0", "seq_1", "expert")

epsilon = 1e-06
very_negative = -1e30
bf16 = jnp.bfloat16
f32 = jnp.float32


def iota(shape, dimension):
    return lax.broadcasted_iota(jnp.int32, shape, dimension)


def mul(a, b):
    return jnp.dot(a, b, preferred_element_type=f32)


def mul_over_last(a, b):
    return lax.dot_general(a, b, (((1,), (1,)), ((), ())), preferred_element_type=f32)


def rms_scale(inputs, gain_vector):
    widened = inputs.astype(f32)
    return (
        widened
        * lax.rsqrt(jnp.mean(widened * widened, axis=-1, keepdims=True) + epsilon)
        * gain_vector
    )


def in_head(shape, h):
    lane = iota(shape, len(shape) - 1)
    return (lane >= h * HEAD) & (lane < (h + 1) * HEAD)


def step_kernel(
    sizes,
    states_hbm,
    flags_hbm,
    ids_hbm,
    enc_gain_hbm,
    moe_gain_hbm,
    dec_gain_hbm,
    w_router_hbm,
    w_in_hbm,
    w_down,
    w_qkv_hbm,
    w_out_hbm,
    w_xq_hbm,
    w_xkv_hbm,
    w_up_hbm,
    w_dq_hbm,
    w_dkv_hbm,
    w_do_hbm,
    bytes_out,
    patch_out,
    states,
    flags,
    ids,
    enc_gain,
    moe_gain,
    dec_gain,
    w_router,
    w_in,
    w_qkv,
    w_out,
    w_xq,
    w_xkv,
    w_up,
    w_dq,
    w_dkv,
    w_do,
    up_held,
    down_0,
    down_1,
    halo,
    keys,
    values,
    mixing,
    routed,
    landed,
    slots,
    hidden,
    sending_0,
    sending_1,
    arriving_0,
    arriving_1,
    leaving,
    returned,
    fetch_sem,
    halo_send,
    halo_recv,
    weight_send,
    weight_recv,
    out_send,
    out_recv,
    gather_send,
    gather_recv,
    ring_send,
    ring_recv,
    back_send,
    back_recv,
):
    groups, ring, peers = sizes
    mesh_id = pl.DeviceIdType.MESH
    plane = lax.axis_index("seq_0")
    at = lax.axis_index("seq_1")
    me = lax.axis_index("expert")
    right = {"seq_1": lax.rem(at + 1, ring)}
    left = {"seq_1": lax.rem(at + ring - 1, ring)}
    up = {"seq_0": lax.rem(plane + 1, groups)}
    down = {"seq_0": lax.rem(plane + groups - 1, groups)}
    count, width = states.shape
    slot_count, outer = patch_out.shape
    share = w_down.shape[0]
    capacity = slots.shape[1] // peers
    rows = peers * capacity
    down_held = (down_0, down_1)
    sending = (sending_0, sending_1)
    arriving = (arriving_0, arriving_1)
    bases = [sum(PARTS[:part]) for part in range(len(PARTS))]
    half = ring // 2

    def peer(j):
        return {"expert": lax.rem(me + j, peers)}

    def stretch(by):
        moved = me + by + peers
        row = at + moved // peers - 1 + ring
        return {
            "seq_0": lax.rem(plane + row // ring - 1 + groups, groups),
            "seq_1": lax.rem(row, ring),
            "expert": lax.rem(moved, peers),
        }

    partners = [up, down, right, left] + [peer(j) for j in range(1, peers)]
    partners += [stretch(1), stretch(2), stretch(-1), stretch(-2)]
    barrier = pltpu.get_barrier_semaphore()
    for device in partners:
        pl.semaphore_signal(barrier, inc=1, device_id=device, device_id_type=mesh_id)

    fetches = {}
    for number, (name, source, target) in enumerate(
        [
            ("down_0", w_down.at[:, pl.ds(0, PARTS[0])], down_0.at[pl.ds(0, share)]),
            ("states", states_hbm, states),
            ("moe_gain", moe_gain_hbm, moe_gain),
            ("w_in", w_in_hbm, w_in),
            ("w_up", w_up_hbm, w_up),
            ("enc_gain", enc_gain_hbm, enc_gain),
            ("qkv", w_qkv_hbm, w_qkv),
            ("flags", flags_hbm, flags),
            ("ids", ids_hbm, ids),
            ("out", w_out_hbm, w_out),
            ("xkv", w_xkv_hbm, w_xkv),
            ("xq", w_xq_hbm, w_xq),
            ("router", w_router_hbm, w_router),
            ("dec_gain", dec_gain_hbm, dec_gain),
            ("down_1", w_down.at[:, pl.ds(PARTS[0], PARTS[1])], down_1.at[pl.ds(0, share)]),
            ("dq", w_dq_hbm, w_dq),
            ("dkv", w_dkv_hbm, w_dkv),
            ("do", w_do_hbm, w_do),
        ]
    ):
        fetches[name] = pltpu.make_async_copy(source, target, fetch_sem.at[number])
    late = ("dq", "dkv", "do")
    for name in fetches:
        if name not in late:
            fetches[name].start()
    pl.semaphore_wait(barrier, len(partners))

    started = []

    def remote(source, target, send, recv, device):
        copy = pltpu.make_async_remote_copy(
            src_ref=source,
            dst_ref=target,
            send_sem=send,
            recv_sem=recv,
            device_id=device,
            device_id_type=mesh_id,
        )
        copy.start()
        started.append(copy)
        return copy

    near = remote(states_hbm, halo.at[1], halo_send.at[0], halo_recv.at[0], stretch(1))
    far = remote(states_hbm, halo.at[0], halo_send.at[1], halo_recv.at[1], stretch(2))

    def weight_copy(stage, direction, source, target):
        return remote(
            source,
            target,
            weight_send.at[direction, stage],
            weight_recv.at[direction, stage],
            up if direction == 0 else down,
        )

    def up_slice(slot):
        return up_held.at[:, pl.ds(slot * share, share)]

    def down_slice(slot, part, rows_from=0, rows_count=None):
        return down_held[part].at[pl.ds(slot * share + rows_from, rows_count or share)]

    def pass_up_first():
        return [weight_copy(0, d, up_slice(0), up_slice((1, 3)[d])) for d in range(2)]

    def pass_up_second():
        copies = []
        for d in range(2):
            begin = up_held.at[d, pl.ds((1, 3)[d] * share, share)]
            copies.append(weight_copy(1, d, begin, up_held.at[d, pl.ds(2 * share, share)]))
        return copies

    def pass_down_first(part):
        source = down_slice(0, part)
        return [
            weight_copy(2 + 2 * part, d, source, down_slice((1, 3)[d], part)) for d in range(2)
        ]

    def pass_down_second(part):
        return [
            weight_copy(
                3 + 2 * part,
                d,
                down_slice((1, 3)[d], part, d * (share // 2), share // 2),
                down_slice(2, part, d * (share // 2), share // 2),
            )
            for d in range(2)
        ]

    def landed_all(copies):
        for copy in copies:
            copy.wait_recv()

    fetches["down_0"].wait()
    down_first = pass_down_first(0)
    for name in ("moe_gain", "w_in", "w_up"):
        fetches[name].wait()
    scaled = (w_in[...].astype(f32) * moe_gain[...]).astype(bf16)
    folded = mul_over_last(scaled, w_up[...]).astype(bf16)
    up_held[0, pl.ds(0, share)] = folded[:share]
    up_held[1, pl.ds(0, share)] = folded[share:]
    up_first = pass_up_first()

    def keep_pairs(number, projected):
        kept = projected.astype(bf16)
        keys[number] = kept[:, :width]
        values[number] = kept[:, width:]

    for name in ("states", "enc_gain", "qkv"):
        fetches[name].wait()
    normed = rms_scale(states[...], enc_gain[...]).astype(bf16)
    queries = (mul(normed, w_qkv[:, pl.ds(0, width)]).astype(bf16).astype(f32) * 0.125).astype(bf16)
    keep_pairs(2, mul(normed, w_qkv[:, pl.ds(width, 2 * width)]))
    near.wait_recv()
    earlier = rms_scale(halo[1], enc_gain[...]).astype(bf16)
    keep_pairs(1, mul(earlier, w_qkv[:, pl.ds(width, 2 * width)]))
    far.wait_recv()
    earlier = rms_scale(halo[0], enc_gain[...]).astype(bf16)
    keep_pairs(0, mul(earlier, w_qkv[:, pl.ds(width, 2 * width)]))

    place = (plane * ring + at) * peers + me
    no_near = jnp.where(place < 1, very_negative, 0.0).astype(f32)
    no_far = jnp.where(place < 2, very_negative, 0.0).astype(f32)
    causal = iota((count, count), 1) <= iota((count, count), 0)
    first_half = iota((count, PAIR), 1) < HEAD
    for pair in range(HEADS // 2):
        columns = slice(pair * PAIR, (pair + 1) * PAIR)
        outs = []
        for side in range(2):
            asked = jnp.where(first_half == (side == 0), queries[:, columns].astype(f32), 0.0)
            asked = asked.astype(bf16)
            own = mul_over_last(asked, keys[2, :, columns])
            back_two = mul_over_last(asked, keys[0, :, columns]) + no_far
            back_one = mul_over_last(asked, keys[1, :, columns]) + no_near
            shared = jnp.where(causal, own, back_two)
            highest = jnp.maximum(
                jnp.max(shared, axis=-1, keepdims=True), jnp.max(back_one, axis=-1, keepdims=True)
            )
            shared = jnp.exp(shared - highest)
            back_one = jnp.exp(back_one - highest)
            total = jnp.sum(shared, axis=-1, keepdims=True) + jnp.sum(
                back_one, axis=-1, keepdims=True
            )
            mixed = (
                mul(jnp.where(causal, shared, 0.0).astype(bf16), values[2, :, columns])
                + mul(jnp.where(causal, 0.0, shared).astype(bf16), values[0, :, columns])
                + mul(back_one.astype(bf16), values[1, :, columns])
            )
            outs.append(mixed / total)
        mixing[:, columns] = jnp.where(first_half, outs[0], outs[1]).astype(bf16)
        if pair == 1:
            landed_all(down_first)
            down_second = pass_down_second(0)
    fetches["out"].wait()
    for name in late:
        fetches[name].start()
    encoded = (states[...].astype(f32) + mul(mixing[...], w_out[...])).astype(bf16)

    fetches["flags"].wait()
    opened = flags[...].astype(f32)
    row_at = iota((count, count), 0)
    column_at = iota((count, count), 1)
    opened_wide = jnp.broadcast_to(opened, (8, count)).astype(bf16)
    number_row = mul(opened_wide, (row_at <= column_at).astype(f32).astype(bf16))[:1] - 1.0
    next_row = mul(opened_wide, (row_at <= column_at + 1).astype(f32).astype(bf16))[:1] - 1.0
    last_row = (next_row > number_row) | (iota((1, count), 1) == count - 1)
    seen = (column_at <= row_at) & (opened > 0.5)
    number_column = jnp.sum(seen.astype(f32), axis=1, keepdims=True) - 1.0
    begin = jnp.max(jnp.where(seen, column_at, -1).astype(f32), axis=1, keepdims=True)
    depth = iota((count, 1), 0).astype(f32) - begin
    scanned = encoded.astype(f32)
    reach = 1
    while reach < count:
        moved = pltpu.roll(scanned, reach, 0)
        scanned = jnp.where(depth >= reach, jnp.maximum(scanned, moved), scanned)
        reach *= 2
    member = iota((slot_count, count), 0).astype(f32) == number_row
    live = jnp.max(member.astype(f32), axis=1, keepdims=True)
    chosen_last = jnp.where(member & last_row, 1.0, 0.0).astype(bf16)
    pooled = mul(chosen_last, scanned.astype(bf16))
    fetches["xkv"].wait()
    pairs = mul(encoded, w_xkv[...]).astype(bf16)
    fetches["xq"].wait()
    asked = mul(pooled.astype(bf16), w_xq[...]).astype(bf16).astype(f32) * 0.125
    stacked = jnp.concatenate(
        [jnp.where(in_head(asked.shape, h), asked, 0.0) for h in range(HEADS)], axis=0
    ).astype(bf16)
    bias = jnp.where(member, 0.0, very_negative)
    scores = mul_over_last(stacked, pairs[:, :width]) + jnp.concatenate([bias] * HEADS, axis=0)
    raised = jnp.exp(scores - jnp.max(scores, axis=-1, keepdims=True))
    weighed = (raised / jnp.sum(raised, axis=-1, keepdims=True)).astype(bf16)
    spread_out = mul(weighed, pairs[:, width:])
    patch_mix = pooled
    for h in range(HEADS):
        part = spread_out[h * slot_count : (h + 1) * slot_count]
        patch_mix = patch_mix + jnp.where(in_head(part.shape, h), part, 0.0)
    patch_input = jnp.where(live > 0.5, patch_mix, 0.0).astype(bf16)
    state = mul(patch_input, w_up[...]).astype(bf16).astype(f32)
    scale = lax.rsqrt(jnp.mean(state * state, axis=-1, keepdims=True) + epsilon)

    lane = iota((slot_count, peers * PADDED), 1)
    fetches["ids"].wait()
    same = iota((slot_count,) * 2, 0) == iota((slot_count,) * 2, 1)
    ids_row = [ids[k : k + 1].astype(f32) for k in range(2)]
    expert = [
        jnp.sum(jnp.where(same, row, 0.0), axis=1, keepdims=True).astype(jnp.int32)
        for row in ids_row
    ]
    named = [jnp.where(lane == expert[k], 1.0, 0.0) for k in range(2)]
    before = jnp.where(iota((slot_count,) * 2, 1) < iota((slot_count,) * 2, 0), 1.0, 0.0)
    counted = mul(before.astype(bf16), (named[0] + named[1]).astype(bf16))
    target = []
    for k in range(2):
        rank = jnp.sum(counted * named[k], axis=1, keepdims=True).astype(jnp.int32)
        relative = expert[k] - me
        relative = jnp.where(relative < 0, relative + peers, relative)
        target.append(relative * PADDED + rank)
    placed = jnp.where((lane == target[0]) | (lane == target[1]), 1.0, 0.0)
    sent = (patch_input.astype(f32) * scale).astype(bf16)
    routed[...] = mul(jnp.transpose(placed).astype(bf16), sent).astype(bf16)

    outward = [
        remote(
            routed.at[pl.ds(j * PADDED, PADDED)],
            landed.at[pl.ds(j * PADDED, PADDED)],
            out_send.at[j],
            out_recv.at[j],
            peer(j),
        )
        for j in range(1, peers)
    ]
    landed[pl.ds(0, PADDED)] = routed[pl.ds(0, PADDED)]

    patch_normed = (state * scale * moe_gain[...]).astype(bf16)
    fetches["router"].wait()
    logits = lax.dot_general(
        patch_normed.astype(f32),
        w_router[...],
        (((1,), (1,)), ((), ())),
        precision=lax.Precision.HIGHEST,
        preferred_element_type=f32,
    )
    column = iota(logits.shape, 1)
    picked = [
        jnp.sum(jnp.where(column == expert[k], logits, 0.0), axis=1, keepdims=True)
        for k in range(2)
    ]
    top = jnp.maximum(picked[0], picked[1])
    raised = [jnp.exp(value - top) for value in picked]
    gates = [value / (raised[0] + raised[1]) for value in raised]
    weighted = jnp.where(lane == target[0], gates[0], 0.0) + jnp.where(
        lane == target[1], gates[1], 0.0
    )
    weighted_high = weighted.astype(bf16)
    weighted_low = (weighted - weighted_high.astype(f32)).astype(bf16)
    fetches["dq"].wait()
    fetches["dec_gain"].wait()
    byte_normed = rms_scale(encoded, dec_gain[...]).astype(bf16)
    byte_queries = (mul(byte_normed, w_dq[...]).astype(bf16).astype(f32) * 0.125).astype(bf16)

    def place_of(index):
        return (index >> 4) * capacity + (index & (PADDED - 1))

    def used(index):
        return (index & (PADDED - 1)) < capacity

    wide = iota((rows, peers * PADDED), 1)
    compact = jnp.where((iota(wide.shape, 0) == place_of(wide)) & used(wide), 1.0, 0.0)
    tall = iota((peers * PADDED, rows), 0)
    spread = jnp.where((iota(tall.shape, 1) == place_of(tall)) & used(tall), 1.0, 0.0)
    spread = spread.astype(bf16)

    landed_all(outward)
    slots[0] = mul(compact.astype(bf16), landed[...]).astype(bf16)

    def forward_right(hop):
        if hop < half:
            source, end = slots.at[hop - 1], slots.at[hop]
        else:
            part = pl.ds(0, rows // 2)
            source, end = slots.at[hop - 1, part], slots.at[hop, part]
        return remote(source, end, gather_send.at[0, hop], gather_recv.at[0, hop], right)

    def forward_left(hop):
        begin, finish = (ring - hop + 1) % ring, ring - hop
        if hop < half:
            source, end = slots.at[begin], slots.at[finish]
        else:
            part = pl.ds(rows // 2, rows // 2)
            source, end = slots.at[begin, part], slots.at[finish, part]
        return remote(source, end, gather_send.at[1, hop], gather_recv.at[1, hop], left)

    def fill_hidden(slot):
        block = slots[slot]
        gate = mul_over_last(block, up_held[0])
        upper = mul_over_last(block, up_held[1])
        hidden[slot] = (gate / (1.0 + jnp.exp(-gate)) * upper).astype(bf16)

    def ring_columns(part, direction):
        return pl.ds(bases[part] + direction * (PARTS[part] // 2), PARTS[part] // 2)

    def term(slot, part, direction):
        columns = pl.ds(direction * (PARTS[part] // 2), PARTS[part] // 2)
        return mul(hidden[slot], down_held[part][:, columns])

    pending = {}

    def advance(part, step):
        for direction in range(2):
            total = term(step + 1 if direction == 0 else ring - 1 - step, part, direction)
            for piece in range(PIECES):
                begin = piece * (rows // PIECES)
                piece_rows = pl.ds(begin, rows // PIECES)
                value = total[begin : begin + rows // PIECES]
                if step > 0:
                    pending[part, direction, piece].wait_recv()
                    value = value + arriving[part][direction, step - 1, piece_rows].astype(f32)
                sending[part][direction, step, piece_rows] = value.astype(bf16)
                number = (part * 2 + direction) * PIECES + piece
                pending[part, direction, piece] = remote(
                    sending[part].at[direction, step, piece_rows],
                    arriving[part].at[direction, step, piece_rows],
                    ring_send.at[number, step],
                    ring_recv.at[number, step],
                    right if direction == 0 else left,
                )

    def send_back(part):
        columns = pl.ds(bases[part], PARTS[part])
        for direction in range(2):
            total = term(0, part, direction)
            for piece in range(PIECES):
                pending[part, direction, piece].wait_recv()
            total = (total + arriving[part][direction, ring - 2].astype(f32)).astype(bf16)
            leaving[:, ring_columns(part, direction)] = mul(spread, total).astype(bf16)
        copies = []
        for j in range(1, peers):
            rows_of = pl.ds(j * PADDED, PADDED)
            copies.append(
                remote(
                    leaving.at[rows_of, columns],
                    returned.at[rows_of, columns],
                    back_send.at[part, j],
                    back_recv.at[part, j],
                    peer(peers - j),
                )
            )
        returned[pl.ds(0, PADDED), columns] = leaving[pl.ds(0, PADDED), columns]
        return copies

    to_right, to_left = forward_right(1), forward_left(1)
    landed_all(up_first)
    up_second = pass_up_second()
    fetches["down_1"].wait()
    down_first = pass_down_first(1)
    landed_all(up_second)
    fill_hidden(0)
    back = []
    for tick in range(LAGS[-1] + ring):
        hop = tick + 1
        if hop <= half:
            landed_all([to_right, to_left])
            if hop < half:
                to_right, to_left = forward_right(hop + 1), forward_left(hop + 1)
            fill_hidden(hop)
            if hop < half:
                fill_hidden(ring - hop)
        if tick in LAGS:
            landed_all(down_second)
        if tick + 1 in LAGS:
            part = LAGS.index(tick + 1)
            landed_all(down_first)
            down_second = pass_down_second(part)
            if part + 1 < len(PARTS):
                down_first = pass_down_first(part + 1)
        for part in range(len(PARTS)):
            step = tick - LAGS[part]
            if 0 <= step < ring - 1:
                advance(part, step)
            if step == ring - 1:
                back.append(send_back(part))

    fetches["dkv"].wait()
    pairs = 0.0
    for part in range(len(PARTS)):
        columns = pl.ds(bases[part], PARTS[part])
        landed_all(back[part])
        combined = mul(weighted_high, returned[:, columns]) + mul(
            weighted_low, returned[:, columns]
        )
        finished = state[:, bases[part] : bases[part] + PARTS[part]] + combined
        patch_out[:, columns] = finished
        pairs = pairs + mul(finished.astype(bf16), w_dkv[columns])

    pairs = pairs.astype(bf16).astype(f32)
    nothing = jnp.zeros((PAIR - slot_count, width), f32)

    def by_head(block):
        parts = []
        for h in range(HEADS):
            parts += [jnp.where(in_head(block.shape, h), block, 0.0), nothing]
        return jnp.concatenate(parts, axis=0).astype(bf16)

    scores = mul_over_last(byte_queries, by_head(pairs[:, :width]))
    allowed = iota((count, PAIR), 1).astype(f32) <= number_column
    weighed = []
    for h in range(HEADS):
        part = jnp.where(allowed, scores[:, h * PAIR : (h + 1) * PAIR], very_negative)
        raised = jnp.exp(part - jnp.max(part, axis=-1, keepdims=True))
        weighed.append((raised / jnp.sum(raised, axis=-1, keepdims=True)).astype(bf16))
    mixed = mul(jnp.concatenate(weighed, axis=1), by_head(pairs[:, width:])).astype(bf16)
    fetches["do"].wait()
    bytes_out[...] = encoded.astype(f32) + mul(mixed, w_do[...])
    for copy in started:
        copy.wait_send()


def per_device(
    byte_states,
    patch_start,
    expert_ids,
    enc_gain,
    w_qkv,
    w_out,
    w_xq,
    w_xkv,
    w_up,
    moe_gain,
    w_router,
    w_in,
    w_down,
    dec_gain,
    w_dq,
    w_dkv,
    w_do,
):
    groups, ring, peers = (lax.axis_size(axis) for axis in SEQ_EXPERT)
    count, width = byte_states.shape
    slot_count = expert_ids.shape[0]
    outer = w_up.shape[1]
    share = w_down.shape[1]
    rows = peers * (12 * slot_count // (5 * peers))
    dma = pltpu.SemaphoreType.DMA
    vmem = pltpu.VMEM
    small = [
        byte_states,
        patch_start[None, :],
        expert_ids.T,
        enc_gain[None, :],
        moe_gain[None, :],
        dec_gain[None, :],
        w_router.T,
        jnp.transpose(w_in[0], (1, 2, 0)).reshape(2 * share, outer),
    ]
    weights = [w_qkv, w_out, w_xq, w_xkv, w_up, w_dq, w_dkv, w_do]
    made = pl.pallas_call(
        functools.partial(step_kernel, (groups, ring, peers)),
        out_shape=(
            jax.ShapeDtypeStruct((count, width), f32),
            jax.ShapeDtypeStruct((slot_count, outer), f32),
        ),
        in_specs=[pl.BlockSpec(memory_space=pl.ANY)] * 17,
        out_specs=(pl.BlockSpec(memory_space=pltpu.VMEM),) * 2,
        scratch_shapes=[vmem(w.shape, w.dtype) for w in small + weights]
        + [
            vmem((2, groups * share, width), bf16),
            *[vmem((groups * share, part), bf16) for part in PARTS],
            vmem((2, count, width), bf16),
            vmem((3, count, width), bf16),
            vmem((3, count, width), bf16),
            vmem((count, width), bf16),
            vmem((peers * PADDED, width), bf16),
            vmem((peers * PADDED, width), bf16),
            vmem((ring, rows, width), bf16),
            vmem((ring, rows, groups * share), bf16),
            *[vmem((2, ring - 1, rows, part // 2), bf16) for part in PARTS * 2],
            vmem((peers * PADDED, outer), bf16),
            vmem((peers * PADDED, outer), bf16),
            dma((18,)),
            dma((2,)),
            dma((2,)),
            dma((2, 2 + 2 * len(PARTS))),
            dma((2, 2 + 2 * len(PARTS))),
            dma((peers,)),
            dma((peers,)),
            dma((2, ring // 2 + 1)),
            dma((2, ring // 2 + 1)),
            dma((2 * PIECES * len(PARTS), ring - 1)),
            dma((2 * PIECES * len(PARTS), ring - 1)),
            dma((len(PARTS), peers)),
            dma((len(PARTS), peers)),
        ],
        compiler_params=pltpu.CompilerParams(
            collective_id=0, has_side_effects=True, vmem_limit_bytes=64000000
        ),
    )(*small, w_down[0], *weights)
    return tuple(value.astype(bf16) for value in made)


def solution(mesh):
    split = Mesh(mesh.devices.reshape(4, 8, mesh.shape["expert"]), SEQ_EXPERT)
    placed = (
        P(SEQ_EXPERT, None),
        P(SEQ_EXPERT),
        P(SEQ_EXPERT, None),
        P(),
        P(),
        P(),
        P(),
        P(),
        P(),
        P(),
        P(),
        P("expert", None, None, SEQ),
        P("expert", SEQ, None),
        P(),
        P(),
        P(),
        P(),
    )
    return jax.shard_map(
        per_device,
        mesh=split,
        in_specs=placed,
        out_specs=(P(SEQ_EXPERT, None), P(SEQ_EXPERT, None)),
        check_vma=False,
    )
```

```python
import functools

import jax
import jax.numpy as jnp
from jax import lax
from jax.experimental import pallas as pl
from jax.experimental.pallas import tpu as pltpu
from jax.sharding import Mesh
from jax.sharding import PartitionSpec as P

HEADS = 8
HEAD = 64
PAIR = 2 * HEAD
PADDED = 16
PARTS = (1024, 1024)
LAGS = (0, 2)
PIECES = 2
PASS_AT = 1
SEQ = ("seq_0", "seq_1")
SEQ_EXPERT = ("seq_0", "seq_1", "expert")

epsilon = 1e-06
very_negative = -1e30
bf16 = jnp.bfloat16
f32 = jnp.float32


def iota(shape, dimension):
    return lax.broadcasted_iota(jnp.int32, shape, dimension)


def mul(a, b):
    return jnp.dot(a, b, preferred_element_type=f32)


def mul_over_last(a, b):
    return lax.dot_general(a, b, (((1,), (1,)), ((), ())), preferred_element_type=f32)


def rms_scale(inputs, gain_vector):
    widened = inputs.astype(f32)
    return (
        widened
        * lax.rsqrt(jnp.mean(widened * widened, axis=-1, keepdims=True) + epsilon)
        * gain_vector
    )


def in_head(shape, h):
    lane = iota(shape, len(shape) - 1)
    return (lane >= h * HEAD) & (lane < (h + 1) * HEAD)


def step_kernel(
    sizes,
    states_hbm,
    flags_hbm,
    ids_hbm,
    enc_gain_hbm,
    moe_gain_hbm,
    dec_gain_hbm,
    w_router_hbm,
    w_in_hbm,
    w_down,
    w_qkv_hbm,
    w_out_hbm,
    w_xq_hbm,
    w_xkv_hbm,
    w_up_hbm,
    w_dq_hbm,
    w_dkv_hbm,
    w_do_hbm,
    bytes_out,
    patch_out,
    states,
    flags,
    ids,
    enc_gain,
    moe_gain,
    dec_gain,
    w_router,
    w_in,
    w_qkv,
    w_out,
    w_xq,
    w_xkv,
    w_up,
    w_dq,
    w_dkv,
    w_do,
    up_held,
    down_0,
    down_1,
    halo,
    keys,
    values,
    mixing,
    routed,
    landed,
    slots,
    hidden,
    sending_0,
    sending_1,
    arriving_0,
    arriving_1,
    leaving,
    returned,
    fetch_sem,
    halo_send,
    halo_recv,
    weight_send,
    weight_recv,
    out_send,
    out_recv,
    gather_send,
    gather_recv,
    ring_send,
    ring_recv,
    back_send,
    back_recv,
):
    groups, ring, peers = sizes
    mesh_id = pl.DeviceIdType.MESH
    plane = lax.axis_index("seq_0")
    at = lax.axis_index("seq_1")
    me = lax.axis_index("expert")
    right = {"seq_1": lax.rem(at + 1, ring)}
    left = {"seq_1": lax.rem(at + ring - 1, ring)}
    up = {"seq_0": lax.rem(plane + 1, groups)}
    down = {"seq_0": lax.rem(plane + groups - 1, groups)}
    count, width = states.shape
    slot_count, outer = patch_out.shape
    share = w_down.shape[0]
    capacity = slots.shape[1] // peers
    rows = peers * capacity
    down_held = (down_0, down_1)
    sending = (sending_0, sending_1)
    arriving = (arriving_0, arriving_1)
    bases = [sum(PARTS[:part]) for part in range(len(PARTS))]
    half = ring // 2

    def peer(j):
        return {"expert": lax.rem(me + j, peers)}

    def stretch(by):
        moved = me + by + peers
        row = at + moved // peers - 1 + ring
        return {
            "seq_0": lax.rem(plane + row // ring - 1 + groups, groups),
            "seq_1": lax.rem(row, ring),
            "expert": lax.rem(moved, peers),
        }

    partners = [up, down, right, left] + [peer(j) for j in range(1, peers)]
    partners += [stretch(1), stretch(2), stretch(-1), stretch(-2)]
    barrier = pltpu.get_barrier_semaphore()
    for device in partners:
        pl.semaphore_signal(barrier, inc=1, device_id=device, device_id_type=mesh_id)

    fetches = {}
    for number, (name, source, target) in enumerate(
        [
            ("down_0", w_down.at[:, pl.ds(0, PARTS[0])], down_0.at[pl.ds(0, share)]),
            ("states", states_hbm, states),
            ("moe_gain", moe_gain_hbm, moe_gain),
            ("w_in", w_in_hbm, w_in),
            ("w_up", w_up_hbm, w_up),
            ("enc_gain", enc_gain_hbm, enc_gain),
            ("qkv", w_qkv_hbm, w_qkv),
            ("flags", flags_hbm, flags),
            ("ids", ids_hbm, ids),
            ("out", w_out_hbm, w_out),
            ("xkv", w_xkv_hbm, w_xkv),
            ("xq", w_xq_hbm, w_xq),
            ("router", w_router_hbm, w_router),
            ("dec_gain", dec_gain_hbm, dec_gain),
            ("down_1", w_down.at[:, pl.ds(PARTS[0], PARTS[1])], down_1.at[pl.ds(0, share)]),
            ("dq", w_dq_hbm, w_dq),
            ("dkv", w_dkv_hbm, w_dkv),
            ("do", w_do_hbm, w_do),
        ]
    ):
        fetches[name] = pltpu.make_async_copy(source, target, fetch_sem.at[number])
    late = ("dq", "dkv", "do")
    for name in fetches:
        if name not in late:
            fetches[name].start()
    pl.semaphore_wait(barrier, len(partners))

    started = []

    def remote(source, target, send, recv, device):
        copy = pltpu.make_async_remote_copy(
            src_ref=source,
            dst_ref=target,
            send_sem=send,
            recv_sem=recv,
            device_id=device,
            device_id_type=mesh_id,
        )
        copy.start()
        started.append(copy)
        return copy

    near = remote(states_hbm, halo.at[1], halo_send.at[0], halo_recv.at[0], stretch(1))
    far = remote(states_hbm, halo.at[0], halo_send.at[1], halo_recv.at[1], stretch(2))

    def weight_copy(stage, direction, source, target):
        return remote(
            source,
            target,
            weight_send.at[direction, stage],
            weight_recv.at[direction, stage],
            up if direction == 0 else down,
        )

    def up_slice(slot):
        return up_held.at[:, pl.ds(slot * share, share)]

    def down_slice(slot, part, rows_from=0, rows_count=None):
        return down_held[part].at[pl.ds(slot * share + rows_from, rows_count or share)]

    def pass_up_first():
        return [weight_copy(0, d, up_slice(0), up_slice((1, 3)[d])) for d in range(2)]

    def pass_up_second():
        copies = []
        for d in range(2):
            begin = up_held.at[d, pl.ds((1, 3)[d] * share, share)]
            copies.append(weight_copy(1, d, begin, up_held.at[d, pl.ds(2 * share, share)]))
        return copies

    def pass_down_first(part):
        source = down_slice(0, part)
        return [
            weight_copy(2 + 2 * part, d, source, down_slice((1, 3)[d], part)) for d in range(2)
        ]

    def pass_down_second(part):
        return [
            weight_copy(
                3 + 2 * part,
                d,
                down_slice((1, 3)[d], part, d * (share // 2), share // 2),
                down_slice(2, part, d * (share // 2), share // 2),
            )
            for d in range(2)
        ]

    def landed_all(copies):
        for copy in copies:
            copy.wait_recv()

    fetches["down_0"].wait()
    down_first = pass_down_first(0)
    for name in ("moe_gain", "w_in", "w_up"):
        fetches[name].wait()
    scaled = (w_in[...].astype(f32) * moe_gain[...]).astype(bf16)
    folded = mul_over_last(scaled, w_up[...]).astype(bf16)
    up_held[0, pl.ds(0, share)] = folded[:share]
    up_held[1, pl.ds(0, share)] = folded[share:]
    up_first = pass_up_first()

    def keep_pairs(number, projected):
        kept = projected.astype(bf16)
        keys[number] = kept[:, :width]
        values[number] = kept[:, width:]

    for name in ("states", "enc_gain", "qkv"):
        fetches[name].wait()
    normed = rms_scale(states[...], enc_gain[...]).astype(bf16)
    queries = (mul(normed, w_qkv[:, pl.ds(0, width)]).astype(bf16).astype(f32) * 0.125).astype(bf16)
    keep_pairs(2, mul(normed, w_qkv[:, pl.ds(width, 2 * width)]))
    near.wait_recv()
    earlier = rms_scale(halo[1], enc_gain[...]).astype(bf16)
    keep_pairs(1, mul(earlier, w_qkv[:, pl.ds(width, 2 * width)]))
    far.wait_recv()
    earlier = rms_scale(halo[0], enc_gain[...]).astype(bf16)
    keep_pairs(0, mul(earlier, w_qkv[:, pl.ds(width, 2 * width)]))

    place = (plane * ring + at) * peers + me
    no_near = jnp.where(place < 1, very_negative, 0.0).astype(f32)
    no_far = jnp.where(place < 2, very_negative, 0.0).astype(f32)
    causal = iota((count, count), 1) <= iota((count, count), 0)
    first_half = iota((count, PAIR), 1) < HEAD
    for pair in range(HEADS // 2):
        columns = slice(pair * PAIR, (pair + 1) * PAIR)
        outs = []
        for side in range(2):
            asked = jnp.where(first_half == (side == 0), queries[:, columns].astype(f32), 0.0)
            asked = asked.astype(bf16)
            own = mul_over_last(asked, keys[2, :, columns])
            back_two = mul_over_last(asked, keys[0, :, columns]) + no_far
            back_one = mul_over_last(asked, keys[1, :, columns]) + no_near
            shared = jnp.where(causal, own, back_two)
            highest = jnp.maximum(
                jnp.max(shared, axis=-1, keepdims=True), jnp.max(back_one, axis=-1, keepdims=True)
            )
            shared = jnp.exp(shared - highest)
            back_one = jnp.exp(back_one - highest)
            total = jnp.sum(shared, axis=-1, keepdims=True) + jnp.sum(
                back_one, axis=-1, keepdims=True
            )
            mixed = (
                mul(jnp.where(causal, shared, 0.0).astype(bf16), values[2, :, columns])
                + mul(jnp.where(causal, 0.0, shared).astype(bf16), values[0, :, columns])
                + mul(back_one.astype(bf16), values[1, :, columns])
            )
            outs.append(mixed / total)
        mixing[:, columns] = jnp.where(first_half, outs[0], outs[1]).astype(bf16)
        if pair == 1:
            landed_all(down_first)
            down_second = pass_down_second(0)
    fetches["out"].wait()
    for name in late:
        fetches[name].start()
    encoded = (states[...].astype(f32) + mul(mixing[...], w_out[...])).astype(bf16)

    fetches["flags"].wait()
    opened = flags[...].astype(f32)
    row_at = iota((count, count), 0)
    column_at = iota((count, count), 1)
    opened_wide = jnp.broadcast_to(opened, (8, count)).astype(bf16)
    number_row = mul(opened_wide, (row_at <= column_at).astype(f32).astype(bf16))[:1] - 1.0
    next_row = mul(opened_wide, (row_at <= column_at + 1).astype(f32).astype(bf16))[:1] - 1.0
    last_row = (next_row > number_row) | (iota((1, count), 1) == count - 1)
    seen = (column_at <= row_at) & (opened > 0.5)
    number_column = jnp.sum(seen.astype(f32), axis=1, keepdims=True) - 1.0
    begin = jnp.max(jnp.where(seen, column_at, -1).astype(f32), axis=1, keepdims=True)
    depth = iota((count, 1), 0).astype(f32) - begin
    scanned = encoded.astype(f32)
    reach = 1
    while reach < count:
        moved = pltpu.roll(scanned, reach, 0)
        scanned = jnp.where(depth >= reach, jnp.maximum(scanned, moved), scanned)
        reach *= 2
    member = iota((slot_count, count), 0).astype(f32) == number_row
    live = jnp.max(member.astype(f32), axis=1, keepdims=True)
    chosen_last = jnp.where(member & last_row, 1.0, 0.0).astype(bf16)
    pooled = mul(chosen_last, scanned.astype(bf16))
    fetches["xkv"].wait()
    pairs = mul(encoded, w_xkv[...]).astype(bf16)
    fetches["xq"].wait()
    asked = mul(pooled.astype(bf16), w_xq[...]).astype(bf16).astype(f32) * 0.125
    stacked = jnp.concatenate(
        [jnp.where(in_head(asked.shape, h), asked, 0.0) for h in range(HEADS)], axis=0
    ).astype(bf16)
    bias = jnp.where(member, 0.0, very_negative)
    scores = mul_over_last(stacked, pairs[:, :width]) + jnp.concatenate([bias] * HEADS, axis=0)
    raised = jnp.exp(scores - jnp.max(scores, axis=-1, keepdims=True))
    weighed = (raised / jnp.sum(raised, axis=-1, keepdims=True)).astype(bf16)
    spread_out = mul(weighed, pairs[:, width:])
    patch_mix = pooled
    for h in range(HEADS):
        part = spread_out[h * slot_count : (h + 1) * slot_count]
        patch_mix = patch_mix + jnp.where(in_head(part.shape, h), part, 0.0)
    patch_input = jnp.where(live > 0.5, patch_mix, 0.0).astype(bf16)
    state = mul(patch_input, w_up[...]).astype(bf16).astype(f32)
    scale = lax.rsqrt(jnp.mean(state * state, axis=-1, keepdims=True) + epsilon)

    lane = iota((slot_count, peers * PADDED), 1)
    fetches["ids"].wait()
    same = iota((slot_count,) * 2, 0) == iota((slot_count,) * 2, 1)
    ids_row = [ids[k : k + 1].astype(f32) for k in range(2)]
    expert = [
        jnp.sum(jnp.where(same, row, 0.0), axis=1, keepdims=True).astype(jnp.int32)
        for row in ids_row
    ]
    named = [jnp.where(lane == expert[k], 1.0, 0.0) for k in range(2)]
    before = jnp.where(iota((slot_count,) * 2, 1) < iota((slot_count,) * 2, 0), 1.0, 0.0)
    counted = mul(before.astype(bf16), (named[0] + named[1]).astype(bf16))
    target = []
    for k in range(2):
        rank = jnp.sum(counted * named[k], axis=1, keepdims=True).astype(jnp.int32)
        relative = expert[k] - me
        relative = jnp.where(relative < 0, relative + peers, relative)
        target.append(relative * PADDED + rank)
    placed = jnp.where((lane == target[0]) | (lane == target[1]), 1.0, 0.0)
    sent = (patch_input.astype(f32) * scale).astype(bf16)
    routed[...] = mul(jnp.transpose(placed).astype(bf16), sent).astype(bf16)

    outward = [
        remote(
            routed.at[pl.ds(j * PADDED, PADDED)],
            landed.at[pl.ds(j * PADDED, PADDED)],
            out_send.at[j],
            out_recv.at[j],
            peer(j),
        )
        for j in range(1, peers)
    ]
    landed[pl.ds(0, PADDED)] = routed[pl.ds(0, PADDED)]

    landed_all(up_first)
    up_second = pass_up_second()
    fetches["down_1"].wait()
    down_first = pass_down_first(1)

    patch_normed = (state * scale * moe_gain[...]).astype(bf16)
    fetches["router"].wait()
    logits = lax.dot_general(
        patch_normed.astype(f32),
        w_router[...],
        (((1,), (1,)), ((), ())),
        precision=lax.Precision.HIGHEST,
        preferred_element_type=f32,
    )
    column = iota(logits.shape, 1)
    picked = [
        jnp.sum(jnp.where(column == expert[k], logits, 0.0), axis=1, keepdims=True)
        for k in range(2)
    ]
    top = jnp.maximum(picked[0], picked[1])
    raised = [jnp.exp(value - top) for value in picked]
    gates = [value / (raised[0] + raised[1]) for value in raised]
    weighted = jnp.where(lane == target[0], gates[0], 0.0) + jnp.where(
        lane == target[1], gates[1], 0.0
    )
    weighted_high = weighted.astype(bf16)
    weighted_low = (weighted - weighted_high.astype(f32)).astype(bf16)
    fetches["dq"].wait()
    fetches["dec_gain"].wait()
    byte_normed = rms_scale(encoded, dec_gain[...]).astype(bf16)
    byte_queries = (mul(byte_normed, w_dq[...]).astype(bf16).astype(f32) * 0.125).astype(bf16)

    def place_of(index):
        return (index >> 4) * capacity + (index & (PADDED - 1))

    def used(index):
        return (index & (PADDED - 1)) < capacity

    wide = iota((rows, peers * PADDED), 1)
    compact = jnp.where((iota(wide.shape, 0) == place_of(wide)) & used(wide), 1.0, 0.0)
    tall = iota((peers * PADDED, rows), 0)
    spread = jnp.where((iota(tall.shape, 1) == place_of(tall)) & used(tall), 1.0, 0.0)
    spread = spread.astype(bf16)

    landed_all(outward)
    slots[0] = mul(compact.astype(bf16), landed[...]).astype(bf16)

    def forward_right(hop):
        if hop < half:
            source, end = slots.at[hop - 1], slots.at[hop]
        else:
            part = pl.ds(0, rows // 2)
            source, end = slots.at[hop - 1, part], slots.at[hop, part]
        return remote(source, end, gather_send.at[0, hop], gather_recv.at[0, hop], right)

    def forward_left(hop):
        begin, finish = (ring - hop + 1) % ring, ring - hop
        if hop < half:
            source, end = slots.at[begin], slots.at[finish]
        else:
            part = pl.ds(rows // 2, rows // 2)
            source, end = slots.at[begin, part], slots.at[finish, part]
        return remote(source, end, gather_send.at[1, hop], gather_recv.at[1, hop], left)

    def fill_hidden(slot):
        block = slots[slot]
        gate = mul_over_last(block, up_held[0])
        upper = mul_over_last(block, up_held[1])
        hidden[slot] = (gate / (1.0 + jnp.exp(-gate)) * upper).astype(bf16)

    def ring_columns(part, direction):
        return pl.ds(bases[part] + direction * (PARTS[part] // 2), PARTS[part] // 2)

    def term(slot, part, direction):
        columns = pl.ds(direction * (PARTS[part] // 2), PARTS[part] // 2)
        return mul(hidden[slot], down_held[part][:, columns])

    pending = {}

    def advance(part, step):
        for direction in range(2):
            total = term(step + 1 if direction == 0 else ring - 1 - step, part, direction)
            for piece in range(PIECES):
                begin = piece * (rows // PIECES)
                piece_rows = pl.ds(begin, rows // PIECES)
                value = total[begin : begin + rows // PIECES]
                if step > 0:
                    pending[part, direction, piece].wait_recv()
                    value = value + arriving[part][direction, step - 1, piece_rows].astype(f32)
                sending[part][direction, step, piece_rows] = value.astype(bf16)
                number = (part * 2 + direction) * PIECES + piece
                pending[part, direction, piece] = remote(
                    sending[part].at[direction, step, piece_rows],
                    arriving[part].at[direction, step, piece_rows],
                    ring_send.at[number, step],
                    ring_recv.at[number, step],
                    right if direction == 0 else left,
                )

    def send_back(part):
        columns = pl.ds(bases[part], PARTS[part])
        for direction in range(2):
            total = term(0, part, direction)
            for piece in range(PIECES):
                pending[part, direction, piece].wait_recv()
            total = (total + arriving[part][direction, ring - 2].astype(f32)).astype(bf16)
            leaving[:, ring_columns(part, direction)] = mul(spread, total).astype(bf16)
        copies = []
        for j in range(1, peers):
            rows_of = pl.ds(j * PADDED, PADDED)
            copies.append(
                remote(
                    leaving.at[rows_of, columns],
                    returned.at[rows_of, columns],
                    back_send.at[part, j],
                    back_recv.at[part, j],
                    peer(peers - j),
                )
            )
        returned[pl.ds(0, PADDED), columns] = leaving[pl.ds(0, PADDED), columns]
        return copies

    to_right, to_left = forward_right(1), forward_left(1)
    landed_all(up_second)
    fill_hidden(0)
    back = []
    for tick in range(LAGS[-1] + ring):
        hop = tick + 1
        if hop <= half:
            landed_all([to_right, to_left])
            if hop < half:
                to_right, to_left = forward_right(hop + 1), forward_left(hop + 1)
            fill_hidden(hop)
            if hop < half:
                fill_hidden(ring - hop)
        if tick in LAGS:
            landed_all(down_second)
        if tick == PASS_AT:
            landed_all(down_first)
            down_second = pass_down_second(1)
        for part in range(len(PARTS)):
            step = tick - LAGS[part]
            if 0 <= step < ring - 1:
                advance(part, step)
            if step == ring - 1:
                back.append(send_back(part))

    fetches["dkv"].wait()
    pairs = 0.0
    for part in range(len(PARTS)):
        columns = pl.ds(bases[part], PARTS[part])
        landed_all(back[part])
        combined = mul(weighted_high, returned[:, columns]) + mul(
            weighted_low, returned[:, columns]
        )
        finished = state[:, bases[part] : bases[part] + PARTS[part]] + combined
        finished = finished.astype(bf16)
        patch_out[:, columns] = finished
        pairs = pairs + mul(finished, w_dkv[columns])

    pairs = pairs.astype(bf16).astype(f32)
    nothing = jnp.zeros((PAIR - slot_count, width), f32)

    def by_head(block):
        parts = []
        for h in range(HEADS):
            parts += [jnp.where(in_head(block.shape, h), block, 0.0), nothing]
        return jnp.concatenate(parts, axis=0).astype(bf16)

    scores = mul_over_last(byte_queries, by_head(pairs[:, :width]))
    allowed = iota((count, PAIR), 1).astype(f32) <= number_column
    weighed = []
    for h in range(HEADS):
        part = jnp.where(allowed, scores[:, h * PAIR : (h + 1) * PAIR], very_negative)
        raised = jnp.exp(part - jnp.max(part, axis=-1, keepdims=True))
        weighed.append((raised / jnp.sum(raised, axis=-1, keepdims=True)).astype(bf16))
    mixed = mul(jnp.concatenate(weighed, axis=1), by_head(pairs[:, width:])).astype(bf16)
    fetches["do"].wait()
    bytes_out[...] = (encoded.astype(f32) + mul(mixed, w_do[...])).astype(bf16)
    for copy in started:
        copy.wait_send()


def hand_over(bytes_in, patches_in, bytes_out, patches_out):
    bytes_out[...] = bytes_in[...]
    patches_out[...] = patches_in[...]


def per_device(
    byte_states,
    patch_start,
    expert_ids,
    enc_gain,
    w_qkv,
    w_out,
    w_xq,
    w_xkv,
    w_up,
    moe_gain,
    w_router,
    w_in,
    w_down,
    dec_gain,
    w_dq,
    w_dkv,
    w_do,
):
    groups, ring, peers = (lax.axis_size(axis) for axis in SEQ_EXPERT)
    count, width = byte_states.shape
    slot_count = expert_ids.shape[0]
    outer = w_up.shape[1]
    share = w_down.shape[1]
    rows = peers * (12 * slot_count // (5 * peers))
    dma = pltpu.SemaphoreType.DMA
    vmem = pltpu.VMEM
    small = [
        byte_states,
        patch_start[None, :],
        expert_ids.T,
        enc_gain[None, :],
        moe_gain[None, :],
        dec_gain[None, :],
        w_router.T,
        jnp.transpose(w_in[0], (1, 2, 0)).reshape(2 * share, outer),
    ]
    weights = [w_qkv, w_out, w_xq, w_xkv, w_up, w_dq, w_dkv, w_do]
    made = pl.pallas_call(
        functools.partial(step_kernel, (groups, ring, peers)),
        out_shape=(
            jax.ShapeDtypeStruct((count, width), bf16),
            jax.ShapeDtypeStruct((slot_count, outer), bf16),
        ),
        in_specs=[pl.BlockSpec(memory_space=pl.ANY)] * 17,
        out_specs=(pl.BlockSpec(memory_space=pltpu.VMEM),) * 2,
        scratch_shapes=[vmem(w.shape, w.dtype) for w in small + weights]
        + [
            vmem((2, groups * share, width), bf16),
            *[vmem((groups * share, part), bf16) for part in PARTS],
            vmem((2, count, width), bf16),
            vmem((3, count, width), bf16),
            vmem((3, count, width), bf16),
            vmem((count, width), bf16),
            vmem((peers * PADDED, width), bf16),
            vmem((peers * PADDED, width), bf16),
            vmem((ring, rows, width), bf16),
            vmem((ring, rows, groups * share), bf16),
            *[vmem((2, ring - 1, rows, part // 2), bf16) for part in PARTS * 2],
            vmem((peers * PADDED, outer), bf16),
            vmem((peers * PADDED, outer), bf16),
            dma((18,)),
            dma((2,)),
            dma((2,)),
            dma((2, 2 + 2 * len(PARTS))),
            dma((2, 2 + 2 * len(PARTS))),
            dma((peers,)),
            dma((peers,)),
            dma((2, ring // 2 + 1)),
            dma((2, ring // 2 + 1)),
            dma((2 * PIECES * len(PARTS), ring - 1)),
            dma((2 * PIECES * len(PARTS), ring - 1)),
            dma((len(PARTS), peers)),
            dma((len(PARTS), peers)),
        ],
        compiler_params=pltpu.CompilerParams(
            collective_id=0, has_side_effects=True, vmem_limit_bytes=64000000
        ),
    )(*small, w_down[0], *weights)
    return pl.pallas_call(
        hand_over,
        out_shape=tuple(jax.ShapeDtypeStruct(value.shape, bf16) for value in made),
        in_specs=[pl.BlockSpec(memory_space=pltpu.VMEM)] * 2,
        out_specs=(pl.BlockSpec(memory_space=pltpu.VMEM),) * 2,
    )(*made)


def solution(mesh):
    split = Mesh(mesh.devices.reshape(4, 8, mesh.shape["expert"]), SEQ_EXPERT)
    placed = (
        P(SEQ_EXPERT, None),
        P(SEQ_EXPERT),
        P(SEQ_EXPERT, None),
        P(),
        P(),
        P(),
        P(),
        P(),
        P(),
        P(),
        P(),
        P("expert", None, None, SEQ),
        P("expert", SEQ, None),
        P(),
        P(),
        P(),
        P(),
    )
    return jax.shard_map(
        per_device,
        mesh=split,
        in_specs=placed,
        out_specs=(P(SEQ_EXPERT, None), P(SEQ_EXPERT, None)),
        check_vma=False,
    )
```

```python
import functools

import jax
import jax.numpy as jnp
from jax import lax
from jax.experimental import pallas as pl
from jax.experimental.pallas import tpu as pltpu
from jax.sharding import Mesh
from jax.sharding import PartitionSpec as P

HEADS = 8
HEAD = 64
PAIR = 2 * HEAD
PADDED = 16
PARTS = (1024, 1024)
LAGS = (0, 2)
PIECES = 2
PASS_AT = 1
AHEAD = 0
SEQ = ("seq_0", "seq_1")
SEQ_EXPERT = ("seq_0", "seq_1", "expert")

epsilon = 1e-06
very_negative = -1e30
bf16 = jnp.bfloat16
f32 = jnp.float32


def iota(shape, dimension):
    return lax.broadcasted_iota(jnp.int32, shape, dimension)


def mul(a, b):
    return jnp.dot(a, b, preferred_element_type=f32)


def mul_over_last(a, b):
    return lax.dot_general(a, b, (((1,), (1,)), ((), ())), preferred_element_type=f32)


def rms_scale(inputs, gain_vector):
    widened = inputs.astype(f32)
    return (
        widened
        * lax.rsqrt(jnp.mean(widened * widened, axis=-1, keepdims=True) + epsilon)
        * gain_vector
    )


def in_head(shape, h):
    lane = iota(shape, len(shape) - 1)
    return (lane >= h * HEAD) & (lane < (h + 1) * HEAD)


def step_kernel(
    sizes,
    states_hbm,
    flags_hbm,
    ids_hbm,
    enc_gain_hbm,
    moe_gain_hbm,
    dec_gain_hbm,
    w_router_hbm,
    w_in_hbm,
    w_down,
    w_qkv_hbm,
    w_out_hbm,
    w_xq_hbm,
    w_xkv_hbm,
    w_up_hbm,
    w_dq_hbm,
    w_dkv_hbm,
    w_do_hbm,
    bytes_out,
    patch_out,
    states,
    flags,
    ids,
    enc_gain,
    moe_gain,
    dec_gain,
    w_router,
    w_in,
    w_qkv,
    w_out,
    w_xq,
    w_xkv,
    w_up,
    w_dq,
    w_dkv,
    w_do,
    up_held,
    down_0,
    down_1,
    halo,
    keys,
    values,
    mixing,
    routed,
    landed,
    slots,
    hidden,
    sending_0,
    sending_1,
    arriving_0,
    arriving_1,
    leaving,
    returned,
    fetch_sem,
    halo_send,
    halo_recv,
    weight_send,
    weight_recv,
    out_send,
    out_recv,
    gather_send,
    gather_recv,
    ring_send,
    ring_recv,
    back_send,
    back_recv,
):
    groups, ring, peers = sizes
    mesh_id = pl.DeviceIdType.MESH
    plane = lax.axis_index("seq_0")
    at = lax.axis_index("seq_1")
    me = lax.axis_index("expert")
    right = {"seq_1": lax.rem(at + 1, ring)}
    left = {"seq_1": lax.rem(at + ring - 1, ring)}
    up = {"seq_0": lax.rem(plane + 1, groups)}
    down = {"seq_0": lax.rem(plane + groups - 1, groups)}
    count, width = states.shape
    slot_count, outer = patch_out.shape
    share = w_down.shape[0]
    capacity = slots.shape[1] // peers
    rows = peers * capacity
    down_held = (down_0, down_1)
    sending = (sending_0, sending_1)
    arriving = (arriving_0, arriving_1)
    bases = [sum(PARTS[:part]) for part in range(len(PARTS))]
    half = ring // 2

    def peer(j):
        return {"expert": lax.rem(me + j, peers)}

    def stretch(by):
        moved = me + by + peers
        row = at + moved // peers - 1 + ring
        return {
            "seq_0": lax.rem(plane + row // ring - 1 + groups, groups),
            "seq_1": lax.rem(row, ring),
            "expert": lax.rem(moved, peers),
        }

    partners = [up, down, right, left] + [peer(j) for j in range(1, peers)]
    partners += [stretch(1), stretch(2), stretch(-1), stretch(-2)]
    barrier = pltpu.get_barrier_semaphore()
    for device in partners:
        pl.semaphore_signal(barrier, inc=1, device_id=device, device_id_type=mesh_id)

    fetches = {}
    for number, (name, source, target) in enumerate(
        [
            ("down_0", w_down.at[:, pl.ds(0, PARTS[0])], down_0.at[pl.ds(0, share)]),
            ("states", states_hbm, states),
            ("moe_gain", moe_gain_hbm, moe_gain),
            ("w_in", w_in_hbm, w_in),
            ("w_up", w_up_hbm, w_up),
            ("enc_gain", enc_gain_hbm, enc_gain),
            ("qkv", w_qkv_hbm, w_qkv),
            ("flags", flags_hbm, flags),
            ("ids", ids_hbm, ids),
            ("out", w_out_hbm, w_out),
            ("xkv", w_xkv_hbm, w_xkv),
            ("xq", w_xq_hbm, w_xq),
            ("router", w_router_hbm, w_router),
            ("dec_gain", dec_gain_hbm, dec_gain),
            ("down_1", w_down.at[:, pl.ds(PARTS[0], PARTS[1])], down_1.at[pl.ds(0, share)]),
            ("dq", w_dq_hbm, w_dq),
            ("dkv", w_dkv_hbm, w_dkv),
            ("do", w_do_hbm, w_do),
        ]
    ):
        fetches[name] = pltpu.make_async_copy(source, target, fetch_sem.at[number])
    late = ("dq", "dkv", "do")
    for name in fetches:
        if name not in late:
            fetches[name].start()
    pl.semaphore_wait(barrier, len(partners))

    started = []

    def remote(source, target, send, recv, device):
        copy = pltpu.make_async_remote_copy(
            src_ref=source,
            dst_ref=target,
            send_sem=send,
            recv_sem=recv,
            device_id=device,
            device_id_type=mesh_id,
        )
        copy.start()
        started.append(copy)
        return copy

    near = remote(states_hbm, halo.at[1], halo_send.at[0], halo_recv.at[0], stretch(1))
    far = remote(states_hbm, halo.at[0], halo_send.at[1], halo_recv.at[1], stretch(2))

    def weight_copy(stage, direction, source, target):
        return remote(
            source,
            target,
            weight_send.at[direction, stage],
            weight_recv.at[direction, stage],
            up if direction == 0 else down,
        )

    def up_slice(slot):
        return up_held.at[:, pl.ds(slot * share, share)]

    def down_slice(slot, part, rows_from=0, rows_count=None):
        return down_held[part].at[pl.ds(slot * share + rows_from, rows_count or share)]

    def pass_up_first():
        return [weight_copy(0, d, up_slice(0), up_slice((1, 3)[d])) for d in range(2)]

    def pass_up_second():
        copies = []
        for d in range(2):
            begin = up_held.at[d, pl.ds((1, 3)[d] * share, share)]
            copies.append(weight_copy(1, d, begin, up_held.at[d, pl.ds(2 * share, share)]))
        return copies

    def pass_down_first(part):
        source = down_slice(0, part)
        return [
            weight_copy(2 + 2 * part, d, source, down_slice((1, 3)[d], part)) for d in range(2)
        ]

    def pass_down_second(part):
        return [
            weight_copy(
                3 + 2 * part,
                d,
                down_slice((1, 3)[d], part, d * (share // 2), share // 2),
                down_slice(2, part, d * (share // 2), share // 2),
            )
            for d in range(2)
        ]

    def landed_all(copies):
        for copy in copies:
            copy.wait_recv()

    fetches["down_0"].wait()
    down_first = pass_down_first(0)
    for name in ("moe_gain", "w_in", "w_up"):
        fetches[name].wait()
    scaled = (w_in[...].astype(f32) * moe_gain[...]).astype(bf16)
    folded = mul_over_last(scaled, w_up[...]).astype(bf16)
    up_held[0, pl.ds(0, share)] = folded[:share]
    up_held[1, pl.ds(0, share)] = folded[share:]
    up_first = pass_up_first()

    def keep_pairs(number, projected):
        kept = projected.astype(bf16)
        keys[number] = kept[:, :width]
        values[number] = kept[:, width:]

    for name in ("states", "enc_gain", "qkv"):
        fetches[name].wait()
    normed = rms_scale(states[...], enc_gain[...]).astype(bf16)
    queries = (mul(normed, w_qkv[:, pl.ds(0, width)]).astype(bf16).astype(f32) * 0.125).astype(bf16)
    keep_pairs(2, mul(normed, w_qkv[:, pl.ds(width, 2 * width)]))
    near.wait_recv()
    earlier = rms_scale(halo[1], enc_gain[...]).astype(bf16)
    keep_pairs(1, mul(earlier, w_qkv[:, pl.ds(width, 2 * width)]))
    far.wait_recv()
    earlier = rms_scale(halo[0], enc_gain[...]).astype(bf16)
    keep_pairs(0, mul(earlier, w_qkv[:, pl.ds(width, 2 * width)]))

    place = (plane * ring + at) * peers + me
    no_near = jnp.where(place < 1, very_negative, 0.0).astype(f32)
    no_far = jnp.where(place < 2, very_negative, 0.0).astype(f32)
    causal = iota((count, count), 1) <= iota((count, count), 0)
    first_half = iota((count, PAIR), 1) < HEAD
    for pair in range(HEADS // 2):
        columns = slice(pair * PAIR, (pair + 1) * PAIR)
        outs = []
        for side in range(2):
            asked = jnp.where(first_half == (side == 0), queries[:, columns].astype(f32), 0.0)
            asked = asked.astype(bf16)
            own = mul_over_last(asked, keys[2, :, columns])
            back_two = mul_over_last(asked, keys[0, :, columns]) + no_far
            back_one = mul_over_last(asked, keys[1, :, columns]) + no_near
            shared = jnp.where(causal, own, back_two)
            highest = jnp.maximum(
                jnp.max(shared, axis=-1, keepdims=True), jnp.max(back_one, axis=-1, keepdims=True)
            )
            shared = jnp.exp(shared - highest)
            back_one = jnp.exp(back_one - highest)
            total = jnp.sum(shared, axis=-1, keepdims=True) + jnp.sum(
                back_one, axis=-1, keepdims=True
            )
            mixed = (
                mul(jnp.where(causal, shared, 0.0).astype(bf16), values[2, :, columns])
                + mul(jnp.where(causal, 0.0, shared).astype(bf16), values[0, :, columns])
                + mul(back_one.astype(bf16), values[1, :, columns])
            )
            outs.append(mixed / total)
        mixing[:, columns] = jnp.where(first_half, outs[0], outs[1]).astype(bf16)
        if pair == 1:
            landed_all(down_first)
            down_second = pass_down_second(0)
    fetches["out"].wait()
    for name in late:
        fetches[name].start()
    encoded = (states[...].astype(f32) + mul(mixing[...], w_out[...])).astype(bf16)

    fetches["flags"].wait()
    opened = flags[...].astype(f32)
    row_at = iota((count, count), 0)
    column_at = iota((count, count), 1)
    opened_wide = jnp.broadcast_to(opened, (8, count)).astype(bf16)
    number_row = mul(opened_wide, (row_at <= column_at).astype(f32).astype(bf16))[:1] - 1.0
    next_row = mul(opened_wide, (row_at <= column_at + 1).astype(f32).astype(bf16))[:1] - 1.0
    last_row = (next_row > number_row) | (iota((1, count), 1) == count - 1)
    seen = (column_at <= row_at) & (opened > 0.5)
    number_column = jnp.sum(seen.astype(f32), axis=1, keepdims=True) - 1.0
    begin = jnp.max(jnp.where(seen, column_at, -1).astype(f32), axis=1, keepdims=True)
    depth = iota((count, 1), 0).astype(f32) - begin
    scanned = encoded.astype(f32)
    reach = 1
    while reach < count:
        moved = pltpu.roll(scanned, reach, 0)
        scanned = jnp.where(depth >= reach, jnp.maximum(scanned, moved), scanned)
        reach *= 2
    member = iota((slot_count, count), 0).astype(f32) == number_row
    live = jnp.max(member.astype(f32), axis=1, keepdims=True)
    chosen_last = jnp.where(member & last_row, 1.0, 0.0).astype(bf16)
    pooled = mul(chosen_last, scanned.astype(bf16))
    fetches["xkv"].wait()
    pairs = mul(encoded, w_xkv[...]).astype(bf16)
    fetches["xq"].wait()
    asked = mul(pooled.astype(bf16), w_xq[...]).astype(bf16).astype(f32) * 0.125
    stacked = jnp.concatenate(
        [jnp.where(in_head(asked.shape, h), asked, 0.0) for h in range(HEADS)], axis=0
    ).astype(bf16)
    bias = jnp.where(member, 0.0, very_negative)
    scores = mul_over_last(stacked, pairs[:, :width]) + jnp.concatenate([bias] * HEADS, axis=0)
    raised = jnp.exp(scores - jnp.max(scores, axis=-1, keepdims=True))
    weighed = (raised / jnp.sum(raised, axis=-1, keepdims=True)).astype(bf16)
    spread_out = mul(weighed, pairs[:, width:])
    patch_mix = pooled
    for h in range(HEADS):
        part = spread_out[h * slot_count : (h + 1) * slot_count]
        patch_mix = patch_mix + jnp.where(in_head(part.shape, h), part, 0.0)
    patch_input = jnp.where(live > 0.5, patch_mix, 0.0).astype(bf16)
    state = mul(patch_input, w_up[...]).astype(bf16).astype(f32)
    scale = lax.rsqrt(jnp.mean(state * state, axis=-1, keepdims=True) + epsilon)

    lane = iota((slot_count, peers * PADDED), 1)
    fetches["ids"].wait()
    same = iota((slot_count,) * 2, 0) == iota((slot_count,) * 2, 1)
    ids_row = [ids[k : k + 1].astype(f32) for k in range(2)]
    expert = [
        jnp.sum(jnp.where(same, row, 0.0), axis=1, keepdims=True).astype(jnp.int32)
        for row in ids_row
    ]
    named = [jnp.where(lane == expert[k], 1.0, 0.0) for k in range(2)]
    before = jnp.where(iota((slot_count,) * 2, 1) < iota((slot_count,) * 2, 0), 1.0, 0.0)
    counted = mul(before.astype(bf16), (named[0] + named[1]).astype(bf16))
    target = []
    for k in range(2):
        rank = jnp.sum(counted * named[k], axis=1, keepdims=True).astype(jnp.int32)
        relative = expert[k] - me
        relative = jnp.where(relative < 0, relative + peers, relative)
        target.append(relative * PADDED + rank)
    placed = jnp.where((lane == target[0]) | (lane == target[1]), 1.0, 0.0)
    sent = (patch_input.astype(f32) * scale).astype(bf16)
    routed[...] = mul(jnp.transpose(placed).astype(bf16), sent).astype(bf16)

    outward = [
        remote(
            routed.at[pl.ds(j * PADDED, PADDED)],
            landed.at[pl.ds(j * PADDED, PADDED)],
            out_send.at[j],
            out_recv.at[j],
            peer(j),
        )
        for j in range(1, peers)
    ]
    landed[pl.ds(0, PADDED)] = routed[pl.ds(0, PADDED)]

    landed_all(up_first)
    up_second = pass_up_second()
    fetches["down_1"].wait()
    down_first = pass_down_first(1)

    patch_normed = (state * scale * moe_gain[...]).astype(bf16)
    fetches["router"].wait()
    logits = lax.dot_general(
        patch_normed.astype(f32),
        w_router[...],
        (((1,), (1,)), ((), ())),
        precision=lax.Precision.HIGHEST,
        preferred_element_type=f32,
    )
    column = iota(logits.shape, 1)
    picked = [
        jnp.sum(jnp.where(column == expert[k], logits, 0.0), axis=1, keepdims=True)
        for k in range(2)
    ]
    top = jnp.maximum(picked[0], picked[1])
    raised = [jnp.exp(value - top) for value in picked]
    gates = [value / (raised[0] + raised[1]) for value in raised]
    weighted = jnp.where(lane == target[0], gates[0], 0.0) + jnp.where(
        lane == target[1], gates[1], 0.0
    )
    weighted_high = weighted.astype(bf16)
    weighted_low = (weighted - weighted_high.astype(f32)).astype(bf16)
    fetches["dq"].wait()
    fetches["dec_gain"].wait()
    byte_normed = rms_scale(encoded, dec_gain[...]).astype(bf16)
    byte_queries = (mul(byte_normed, w_dq[...]).astype(bf16).astype(f32) * 0.125).astype(bf16)

    def place_of(index):
        return (index >> 4) * capacity + (index & (PADDED - 1))

    def used(index):
        return (index & (PADDED - 1)) < capacity

    wide = iota((rows, peers * PADDED), 1)
    compact = jnp.where((iota(wide.shape, 0) == place_of(wide)) & used(wide), 1.0, 0.0)
    tall = iota((peers * PADDED, rows), 0)
    spread = jnp.where((iota(tall.shape, 1) == place_of(tall)) & used(tall), 1.0, 0.0)
    spread = spread.astype(bf16)

    landed_all(outward)
    slots[0] = mul(compact.astype(bf16), landed[...]).astype(bf16)

    def forward_right(hop):
        if hop < half:
            source, end = slots.at[hop - 1], slots.at[hop]
        else:
            part = pl.ds(0, rows // 2)
            source, end = slots.at[hop - 1, part], slots.at[hop, part]
        return remote(source, end, gather_send.at[0, hop], gather_recv.at[0, hop], right)

    def forward_left(hop):
        begin, finish = (ring - hop + 1) % ring, ring - hop
        if hop < half:
            source, end = slots.at[begin], slots.at[finish]
        else:
            part = pl.ds(rows // 2, rows // 2)
            source, end = slots.at[begin, part], slots.at[finish, part]
        return remote(source, end, gather_send.at[1, hop], gather_recv.at[1, hop], left)

    def fill_hidden(slot):
        block = slots[slot]
        gate = mul_over_last(block, up_held[0])
        upper = mul_over_last(block, up_held[1])
        hidden[slot] = (gate / (1.0 + jnp.exp(-gate)) * upper).astype(bf16)

    def ring_columns(part, direction):
        return pl.ds(bases[part] + direction * (PARTS[part] // 2), PARTS[part] // 2)

    def term(slot, part, direction):
        columns = pl.ds(direction * (PARTS[part] // 2), PARTS[part] // 2)
        return mul(hidden[slot], down_held[part][:, columns])

    pending = {}

    def advance(part, step):
        for direction in range(2):
            total = term(step + 1 if direction == 0 else ring - 1 - step, part, direction)
            for piece in range(PIECES):
                begin = piece * (rows // PIECES)
                piece_rows = pl.ds(begin, rows // PIECES)
                value = total[begin : begin + rows // PIECES]
                if step > 0:
                    pending[part, direction, piece].wait_recv()
                    value = value + arriving[part][direction, step - 1, piece_rows].astype(f32)
                sending[part][direction, step, piece_rows] = value.astype(bf16)
                number = (part * 2 + direction) * PIECES + piece
                pending[part, direction, piece] = remote(
                    sending[part].at[direction, step, piece_rows],
                    arriving[part].at[direction, step, piece_rows],
                    ring_send.at[number, step],
                    ring_recv.at[number, step],
                    right if direction == 0 else left,
                )

    def send_back(part):
        columns = pl.ds(bases[part], PARTS[part])
        for direction in range(2):
            total = term(0, part, direction)
            for piece in range(PIECES):
                pending[part, direction, piece].wait_recv()
            total = (total + arriving[part][direction, ring - 2].astype(f32)).astype(bf16)
            leaving[:, ring_columns(part, direction)] = mul(spread, total).astype(bf16)
        copies = []
        for j in range(1, peers):
            rows_of = pl.ds(j * PADDED, PADDED)
            copies.append(
                remote(
                    leaving.at[rows_of, columns],
                    returned.at[rows_of, columns],
                    back_send.at[part, j],
                    back_recv.at[part, j],
                    peer(peers - j),
                )
            )
        returned[pl.ds(0, PADDED), columns] = leaving[pl.ds(0, PADDED), columns]
        return copies

    to_right, to_left = forward_right(1), forward_left(1)
    back = []
    for turn in range(AHEAD + LAGS[-1] + ring):
        hop, tick = turn + 1, turn - AHEAD
        if hop <= half:
            landed_all([to_right, to_left])
            if hop < half:
                to_right, to_left = forward_right(hop + 1), forward_left(hop + 1)
            if hop == 1:
                landed_all(up_second)
            fill_hidden(hop)
            if hop < half:
                fill_hidden(ring - hop)
            else:
                fill_hidden(0)
        if tick in LAGS:
            landed_all(down_second)
        if tick == PASS_AT:
            landed_all(down_first)
            down_second = pass_down_second(1)
        for part in range(len(PARTS)):
            step = tick - LAGS[part]
            if 0 <= step < ring - 1:
                advance(part, step)
            if step == ring - 1:
                back.append(send_back(part))

    fetches["dkv"].wait()
    pairs = 0.0
    for part in range(len(PARTS)):
        columns = pl.ds(bases[part], PARTS[part])
        landed_all(back[part])
        combined = mul(weighted_high, returned[:, columns]) + mul(
            weighted_low, returned[:, columns]
        )
        finished = state[:, bases[part] : bases[part] + PARTS[part]] + combined
        finished = finished.astype(bf16)
        patch_out[:, columns] = finished
        pairs = pairs + mul(finished, w_dkv[columns])

    pairs = pairs.astype(bf16).astype(f32)
    nothing = jnp.zeros((PAIR - slot_count, width), f32)

    def by_head(block):
        parts = []
        for h in range(HEADS):
            parts += [jnp.where(in_head(block.shape, h), block, 0.0), nothing]
        return jnp.concatenate(parts, axis=0).astype(bf16)

    scores = mul_over_last(byte_queries, by_head(pairs[:, :width]))
    allowed = iota((count, PAIR), 1).astype(f32) <= number_column
    weighed = []
    for h in range(HEADS):
        part = jnp.where(allowed, scores[:, h * PAIR : (h + 1) * PAIR], very_negative)
        raised = jnp.exp(part - jnp.max(part, axis=-1, keepdims=True))
        weighed.append((raised / jnp.sum(raised, axis=-1, keepdims=True)).astype(bf16))
    mixed = mul(jnp.concatenate(weighed, axis=1), by_head(pairs[:, width:])).astype(bf16)
    fetches["do"].wait()
    bytes_out[...] = (encoded.astype(f32) + mul(mixed, w_do[...])).astype(bf16)
    for copy in started:
        copy.wait_send()


def hand_over(bytes_in, patches_in, bytes_out, patches_out):
    bytes_out[...] = bytes_in[...]
    patches_out[...] = patches_in[...]


def per_device(
    byte_states,
    patch_start,
    expert_ids,
    enc_gain,
    w_qkv,
    w_out,
    w_xq,
    w_xkv,
    w_up,
    moe_gain,
    w_router,
    w_in,
    w_down,
    dec_gain,
    w_dq,
    w_dkv,
    w_do,
):
    groups, ring, peers = (lax.axis_size(axis) for axis in SEQ_EXPERT)
    count, width = byte_states.shape
    slot_count = expert_ids.shape[0]
    outer = w_up.shape[1]
    share = w_down.shape[1]
    rows = peers * (12 * slot_count // (5 * peers))
    dma = pltpu.SemaphoreType.DMA
    vmem = pltpu.VMEM
    small = [
        byte_states,
        patch_start[None, :],
        expert_ids.T,
        enc_gain[None, :],
        moe_gain[None, :],
        dec_gain[None, :],
        w_router.T,
        jnp.transpose(w_in[0], (1, 2, 0)).reshape(2 * share, outer),
    ]
    weights = [w_qkv, w_out, w_xq, w_xkv, w_up, w_dq, w_dkv, w_do]
    made = pl.pallas_call(
        functools.partial(step_kernel, (groups, ring, peers)),
        out_shape=(
            jax.ShapeDtypeStruct((count, width), bf16),
            jax.ShapeDtypeStruct((slot_count, outer), bf16),
        ),
        in_specs=[pl.BlockSpec(memory_space=pl.ANY)] * 17,
        out_specs=(pl.BlockSpec(memory_space=pltpu.VMEM),) * 2,
        scratch_shapes=[vmem(w.shape, w.dtype) for w in small + weights]
        + [
            vmem((2, groups * share, width), bf16),
            *[vmem((groups * share, part), bf16) for part in PARTS],
            vmem((2, count, width), bf16),
            vmem((3, count, width), bf16),
            vmem((3, count, width), bf16),
            vmem((count, width), bf16),
            vmem((peers * PADDED, width), bf16),
            vmem((peers * PADDED, width), bf16),
            vmem((ring, rows, width), bf16),
            vmem((ring, rows, groups * share), bf16),
            *[vmem((2, ring - 1, rows, part // 2), bf16) for part in PARTS * 2],
            vmem((peers * PADDED, outer), bf16),
            vmem((peers * PADDED, outer), bf16),
            dma((18,)),
            dma((2,)),
            dma((2,)),
            dma((2, 2 + 2 * len(PARTS))),
            dma((2, 2 + 2 * len(PARTS))),
            dma((peers,)),
            dma((peers,)),
            dma((2, ring // 2 + 1)),
            dma((2, ring // 2 + 1)),
            dma((2 * PIECES * len(PARTS), ring - 1)),
            dma((2 * PIECES * len(PARTS), ring - 1)),
            dma((len(PARTS), peers)),
            dma((len(PARTS), peers)),
        ],
        compiler_params=pltpu.CompilerParams(
            collective_id=0, has_side_effects=True, vmem_limit_bytes=64000000
        ),
    )(*small, w_down[0], *weights)
    return pl.pallas_call(
        hand_over,
        out_shape=tuple(jax.ShapeDtypeStruct(value.shape, bf16) for value in made),
        in_specs=[pl.BlockSpec(memory_space=pltpu.VMEM)] * 2,
        out_specs=(pl.BlockSpec(memory_space=pltpu.VMEM),) * 2,
    )(*made)


def solution(mesh):
    split = Mesh(mesh.devices.reshape(4, 8, mesh.shape["expert"]), SEQ_EXPERT)
    placed = (
        P(SEQ_EXPERT, None),
        P(SEQ_EXPERT),
        P(SEQ_EXPERT, None),
        P(),
        P(),
        P(),
        P(),
        P(),
        P(),
        P(),
        P(),
        P("expert", None, None, SEQ),
        P("expert", SEQ, None),
        P(),
        P(),
        P(),
        P(),
    )
    return jax.shard_map(
        per_device,
        mesh=split,
        in_specs=placed,
        out_specs=(P(SEQ_EXPERT, None), P(SEQ_EXPERT, None)),
        check_vma=False,
    )
```
